32 devices in a mesh: dp: 16 (over z, y, core), tensor: 2 (over x).
Axes of the slice: x: 2, y: 2, z: 4, core: 2. Of those that a mesh axis runs over, the one named last changes fastest.
Arguments:
- inputs: bfloat16 [4096, 1024], P('dp', 'tensor'), may hold values from -6 to 6
- cotangent: bfloat16 [4096, 1024], P('dp', 'tensor'), may hold values from -6 to 6
- attn_gain: float32 [1024], replicated, may hold values from 0.5 to 1.5
- expert_gain: float32 [1024], replicated, may hold values from 0.5 to 1.5
- query_weight: bfloat16 [1024, 1024], P(None, 'tensor'), may hold values from -0.5 to 0.5
- key_weight: bfloat16 [1024, 512], P(None, 'tensor'), may hold values from -0.5 to 0.5
- value_weight: bfloat16 [1024, 512], P(None, 'tensor'), may hold values from -0.1875 to 0.1875
- output_weight: bfloat16 [1024, 1024], P('tensor'), may hold values from -1.5 to 1.5
- router_weight: bfloat16 [1024, 32], replicated, may hold values from -0.09375 to 0.09375
- gate_weight: bfloat16 [32, 1024, 512], P(None, 'dp', 'tensor'), may hold values from -0.1875 to 0.1875
- up_weight: bfloat16 [32, 1024, 512], P(None, 'dp', 'tensor'), may hold values from -0.1875 to 0.1875
- down_weight: bfloat16 [32, 512, 1024], P(None, 'tensor', 'dp'), may hold values from -2 to 2
- routes: int32 [4096, 8], P('dp'), may hold values from 0 to 31, all different within a row
- lengths: int32 [16, 4], replicated, may hold values from 1 to 128, 224 in all within a row
- placement: int32 [16], replicated, may hold values from 0 to 15, each once
Outputs:
- outputs: bfloat16 [4096, 1024], P('dp', 'tensor')
- input_grad: float32 [4096, 1024], P('dp', 'tensor')
- attn_gain_grad: float32 [1024], P('dp')
- expert_gain_grad: float32 [1024], P('dp')
- query_weight_grad: float32 [1024, 1024], P('dp', 'tensor')
- key_weight_grad: float32 [1024, 512], P('dp', 'tensor')
- value_weight_grad: float32 [1024, 512], P('dp', 'tensor')
- output_weight_grad: float32 [1024, 1024], P('tensor', 'dp')
- router_weight_grad: float32 [1024, 32], P('dp')
- gate_weight_grad: float32 [32, 1024, 512], P(None, 'dp', 'tensor')
- up_weight_grad: float32 [32, 1024, 512], P(None, 'dp', 'tensor')
- down_weight_grad: float32 [32, 512, 1024], P(None, 'tensor', 'dp')
The draws below stay inside these ranges and needn't reach their ends.
Inputs may be any that keep to these rules, and one draw needn't show every extreme that they name: Row s lists the lengths of the 4 sequences of slot s, packed in this order from the slot's first token; each row sums to 224 and its largest entry is 128; the other 32 tokens of a slot are padding. Slot s is processed by dp device placement[s]; rows d * 256 to (d + 1) * 256 - 1 of inputs, cotangent and routes are the tokens of the slot that device d processes. `routes`: each row names 8 different experts; rows of padding are ignored.
All inputs are finite; a program needn't handle non-finite values.
Results may differ from the reference program's by a relative error of at most 0.023.
Values may be sent and summed in bfloat16 or wider, within the bound.
No kernel may reach another device: no remote copies, remote signals or barrier semaphores. Data moves between devices by JAX's collectives and lax.ppermute only.
A program may use at most 256 MiB of HBM per device.

```python
import math
import jax
import jax.numpy as jnp
import numpy as np
from jax import lax

D = 1024
HEADS = 16
KV = 8
HEAD_DIM = 64
FF = 512
NEXP = 32
TOPK = 8
EXP_WIN = 32
SEQ_DEV = 4
TOK_DEV = 256
TOKENS = 4096
CAP = 64
FILL = 224
MOST = 128
N_DP = 16


def block_levels(rng, dims, cuts, least, high):
    loudness, own = 1.0, jax.random.fold_in(rng, 6)
    for dim, shards_of in cuts:
        draws = jnp.exp(jax.random.uniform(jax.random.fold_in(own, dim), (shards_of,), jnp.float32, least / len(cuts), high / len(cuts)))
        loudness = loudness * jnp.repeat(draws, dims[dim] // shards_of).reshape([-1 if axis == dim else 1 for axis in range(len(dims))])
    return loudness


def distinct(key, rows, count, top, lift):
    ranking = jax.random.permutation(jax.random.fold_in(key, 1), count)
    favour = ranking
    for power in range(3):
        favour = favour * favour // count
    favour = favour * lift // count
    chance = jax.random.randint(jax.random.fold_in(key, 2), (rows, count), 0, 4096) + favour
    fixed_rows = jax.random.permutation(jax.random.fold_in(key, 3), rows)[jnp.arange(count) % rows]
    chance = jnp.where(jnp.arange(rows)[:, None] == fixed_rows[None, :], 1 << 14, chance)
    priority = chance * count + jnp.arange(count)
    return lax.top_k(priority.astype(jnp.int32), top)[1].astype(jnp.int32)


def profile(amount, total, reach, lean):
    weights = [(1 << 20) // math.isqrt(standing ** lean) + 1 for standing in range(2, amount + 1)]
    spare, given = total - reach - (amount - 1), [1] * (amount - 1)
    while spare > 0:
        candidates = [i for i in range(amount - 1) if given[i] < reach]
        mass, left = sum([weights[i] for i in candidates]), spare
        for i in candidates:
            extra = min(reach - given[i], max(1, left * weights[i] // mass), spare)
            given[i] = given[i] + extra
            spare = spare - extra
    return np.array([reach] + given)


def uneven_parts(own_key, amount, total, reach, lean):
    if amount == 2:
        one = jax.random.randint(own_key, (), max(1, total - reach), min(reach, total - 1) + 1)
        return jnp.stack([one, total - one])
    tallies = jnp.asarray(profile(amount, total, reach, lean), jnp.int32)
    twos = (amount - 1) // 2
    source_of, sink = tallies[1:1 + 2 * twos:2], tallies[2:2 + 2 * twos:2]
    room = jnp.minimum(source_of - 1, reach - sink)
    passed = jax.random.randint(jax.random.fold_in(own_key, 1), (twos,), 0, 1 << 20) % (room + 1)
    tallies = tallies.at[1:1 + 2 * twos:2].set(source_of - passed).at[2:2 + 2 * twos:2].set(sink + passed)
    return tallies[jax.random.permutation(jax.random.fold_in(own_key, 2), amount)]


def noise(rng, dims, scale, limit, shards=(), kind=jnp.bfloat16):
    values = jax.random.normal(rng, dims, jnp.float32) * scale
    if len(shards) > 0:
        values = block_levels(rng, dims, shards, -0.22, 0.18) * values
    return jnp.clip(values, min=-limit, max=limit).astype(kind)


def setup_inputs(seed: int = 0) -> dict:
    splits = jax.random.split(jax.random.key(seed), 16)
    inputs = noise(splits[0], (TOKENS, D), 1.0, 6.0, ((0, 16), (1, 2)))
    cotangent = noise(splits[1], (TOKENS, D), 1.0, 6.0, ((0, 16), (1, 2)))
    attn_gain = jnp.clip(1.0 + 0.1 * jax.random.normal(splits[2], (D,), jnp.float32), 0.5, 1.5)
    expert_gain = jnp.clip(1.0 + 0.1 * jax.random.normal(splits[3], (D,), jnp.float32), 0.5, 1.5)
    query_weight = noise(splits[4], (D, HEADS * HEAD_DIM), (D // 8) ** -0.5, 0.5, ((1, 2),))
    key_weight = noise(splits[5], (D, KV * HEAD_DIM), (D // 8) ** -0.5, 0.5, ((1, 2),))
    value_weight = noise(splits[6], (D, KV * HEAD_DIM), D ** -0.5, 0.1875, ((1, 2),))
    output_weight = noise(splits[7], (HEADS * HEAD_DIM, D), (max(HEADS * HEAD_DIM // 64, 1)) ** -0.5, 1.5, ((0, 2),))
    router_weight = noise(splits[8], (D, NEXP), (4 * D) ** -0.5, 0.09375)
    gate_weight = noise(splits[9], (EXP_WIN, D, FF), D ** -0.5, 0.1875, ((1, 16), (2, 2)))
    up_weight = noise(splits[10], (EXP_WIN, D, FF), D ** -0.5, 0.1875, ((1, 16), (2, 2)))
    down_weight = noise(splits[11], (EXP_WIN, FF, D), (max(FF // 64, 1)) ** -0.5, 2.0, ((1, 2), (2, 16)))
    routes = distinct(splits[12], TOKENS, NEXP, TOPK, 2048)
    lengths = jax.vmap(lambda own: uneven_parts(own, SEQ_DEV, FILL, MOST, 1))(jax.random.split(splits[13], N_DP)).reshape((N_DP, SEQ_DEV)).astype(jnp.int32)
    placement = jax.random.permutation(splits[14], N_DP).astype(jnp.int32)
    return dict(inputs=inputs, cotangent=cotangent, attn_gain=attn_gain, expert_gain=expert_gain, query_weight=query_weight, key_weight=key_weight, value_weight=value_weight, output_weight=output_weight, router_weight=router_weight, gate_weight=gate_weight, up_weight=up_weight, down_weight=down_weight, routes=routes, lengths=lengths, placement=placement)


EPSILON = 1e-06
ROPE_BASE = 10000.0
PRECISE = lax.Precision.HIGHEST
NEGATIVE = -1e+30

@jax.custom_vjp
def low(v):
    return lax.optimization_barrier(v.astype(jnp.bfloat16)).astype(jnp.float32)

@jax.custom_vjp
def low_back(v):
    return v

def low_keep(v):
    return (low(v), None)

def low_pass(kept, grad):
    return (grad,)

def back_keep(v):
    return (v, None)

def back_low(kept, grad):
    return (low(grad),)
low.defvjp(low_keep, low_pass)
low_back.defvjp(back_keep, back_low)

def product(left, right):
    return jnp.dot(left, right, precision=PRECISE)

def rms_norm(values, gain_vector):
    scale = lax.rsqrt(lax.optimization_barrier(jnp.mean(values * values, axis=-1, keepdims=True)) + EPSILON)
    return values * scale * gain_vector

def rope_tables(positions, half_dim):
    freq_index = jnp.arange(half_dim, dtype=jnp.int32).astype(jnp.float32)
    frequency = jnp.exp(-(2.0 * freq_index / (2.0 * half_dim)) * jnp.log(ROPE_BASE))
    angles = positions.astype(jnp.float32)[:, None] * frequency[None, :]
    return (jnp.cos(angles)[:, None, :], jnp.sin(angles)[:, None, :])

def rotate(values, cos_table, sin_table):
    half_dim = values.shape[-1] // 2
    first_half = values[..., :half_dim]
    second = values[..., half_dim:]
    return jnp.concatenate([first_half * cos_table - second * sin_table, second * cos_table + first_half * sin_table], axis=-1)

def slot_layout(slot_lengths, slot_routes):
    row_count = slot_routes.shape[0]
    top_count = slot_routes.shape[1]
    seq_count = slot_lengths.shape[0]
    seg_ends = jnp.cumsum(slot_lengths).astype(jnp.int32)
    seg_starts = (seg_ends - slot_lengths).astype(jnp.int32)
    row_index = jnp.arange(row_count, dtype=jnp.int32)
    segment = lax.optimization_barrier(jnp.sum((row_index[:, None] >= seg_ends[None, :]).astype(jnp.int32), axis=1)).astype(jnp.int32)
    seg_begins = jnp.concatenate([seg_starts, seg_ends[-1:]]).astype(jnp.int32)
    seg_ids = jnp.arange(seq_count + 1, dtype=jnp.int32)
    begin_row = lax.optimization_barrier(jnp.sum(jnp.where(segment[:, None] == seg_ids[None, :], seg_begins[None, :], 0), axis=1)).astype(jnp.int32)
    positions = row_index - begin_row
    token_live = segment < seq_count
    flat_routes = slot_routes.reshape(row_count * top_count)
    live_pairs = (flat_routes[:, None] == jnp.arange(EXP_WIN, dtype=jnp.int32)[None, :]) & jnp.repeat(token_live, top_count)[:, None]
    live_int = live_pairs.astype(jnp.int32)
    earlier = jnp.cumsum(live_int, axis=0).astype(jnp.int32) - live_int
    slot_place = lax.optimization_barrier(jnp.sum(earlier * live_int, axis=1)).astype(jnp.int32)
    kept_pairs = (lax.optimization_barrier(jnp.sum(live_int, axis=1)) > 0) & (slot_place < CAP)
    slot_index = jnp.where(kept_pairs, flat_routes * CAP + slot_place, -1).astype(jnp.int32).reshape(row_count, top_count)
    return (segment, positions, token_live, slot_index)

def layer(inputs, attn_gain, expert_gain, query_weight, key_weight, value_weight, output_weight, router_weight, gate_weight, up_weight, down_weight, structure):
    allowed, token_live, cos_table, sin_table, dispatch, pick_all, pick_window = structure
    row_count = inputs.shape[0]
    group = HEADS // KV
    normed = low(rms_norm(inputs, attn_gain))
    query_rot = low(rotate(low_back(product(normed, query_weight)).reshape(row_count, HEADS, HEAD_DIM), cos_table, sin_table))
    key_rot = low(rotate(low_back(product(normed, key_weight)).reshape(row_count, KV, HEAD_DIM), cos_table, sin_table))
    value_rows = low_back(low(product(normed, value_weight))).reshape(row_count, KV, HEAD_DIM)
    query_rot = query_rot.reshape(row_count, KV, group, HEAD_DIM)
    scores = low_back(jnp.einsum('qhgd,khd->hgqk', query_rot, key_rot, precision=PRECISE) * (1.0 / HEAD_DIM))
    scores = jnp.where(allowed, scores, NEGATIVE)
    attn_probs = jax.nn.softmax(scores, axis=-1)
    context = jnp.einsum('hgqk,khd->qhgd', low(attn_probs), value_rows, precision=PRECISE).reshape(row_count, HEADS * HEAD_DIM)
    context = low_back(low(context * token_live[:, None]))
    residual = inputs + low_back(product(context, output_weight))
    mixed_rows = low(rms_norm(residual, expert_gain))
    logits = product(mixed_rows, router_weight)
    gate_probs = jax.nn.softmax(jnp.einsum('tkn,tn->tk', pick_all, logits, precision=PRECISE), axis=-1)
    token_gates = jnp.einsum('tk,tke->te', gate_probs, pick_window, precision=PRECISE)
    gate_slot = jnp.einsum('te,tec->ec', token_gates, dispatch.reshape(row_count, EXP_WIN, CAP), precision=PRECISE).reshape(EXP_WIN * CAP)
    slot_in = product(dispatch.T, mixed_rows).reshape(EXP_WIN, CAP, D)
    gate_pre = low_back(jnp.einsum('ecd,edf->ecf', slot_in, gate_weight, precision=PRECISE))
    up_pre = low_back(jnp.einsum('ecd,edf->ecf', slot_in, up_weight, precision=PRECISE))
    hidden = low(jax.nn.silu(gate_pre) * up_pre)
    expert_out = low_back(jnp.einsum('ecf,efd->ecd', hidden, down_weight, precision=PRECISE)).reshape(EXP_WIN * CAP, D)
    return residual + product(dispatch, gate_slot[:, None] * expert_out)

def reference(inputs, cotangent, attn_gain, expert_gain, query_weight, key_weight, value_weight, output_weight, router_weight, gate_weight, up_weight, down_weight, routes, lengths, placement):
    devices = placement.shape[0]
    rank_list = jnp.arange(devices, dtype=jnp.int32)
    holder = lax.optimization_barrier(jnp.sum(jnp.where(placement[None, :] == rank_list[:, None], rank_list[None, :], 0), axis=1)).astype(jnp.int32)
    placed_lengths = jnp.take(lengths, holder, axis=0)
    params = tuple((w.astype(jnp.float32) for w in (attn_gain, expert_gain, query_weight, key_weight, value_weight, output_weight, router_weight, gate_weight, up_weight, down_weight)))
    stacked_inputs = inputs.reshape(devices, TOK_DEV, D)
    stacked_cot = cotangent.reshape(devices, TOK_DEV, D)
    stacked_routes = routes.reshape(devices, TOK_DEV, TOPK)

    def one_slot(totals, pieces):
        slot_inputs, slot_cot, slot_routes, slot_lengths = pieces
        segment, positions, token_live, slot_index = slot_layout(slot_lengths, slot_routes)
        row_index = jnp.arange(TOK_DEV, dtype=jnp.int32)
        allowed = (segment[:, None] == segment[None, :]) & (row_index[None, :] <= row_index[:, None])
        cos_table, sin_table = rope_tables(positions, HEAD_DIM // 2)
        columns = jnp.arange(EXP_WIN * CAP, dtype=jnp.int32)
        dispatch = lax.optimization_barrier(jnp.sum((slot_index[:, :, None] == columns[None, None, :]).astype(jnp.float32), axis=1))
        pick_all = (slot_routes[:, :, None] == jnp.arange(NEXP, dtype=jnp.int32)[None, None, :]).astype(jnp.float32)
        pick_window = (slot_routes[:, :, None] == jnp.arange(EXP_WIN, dtype=jnp.int32)[None, None, :]).astype(jnp.float32)
        structure = (allowed, token_live.astype(jnp.float32), cos_table, sin_table, dispatch, pick_all, pick_window)

        def forward(*values):
            return layer(*values, structure)
        result, pull = jax.vjp(forward, slot_inputs.astype(jnp.float32), *params)
        grads = pull(slot_cot.astype(jnp.float32))
        totals = tuple((a + b for a, b in zip(totals, grads[1:])))
        return (totals, (result.astype(jnp.bfloat16), grads[0]))
    initial = tuple((jnp.zeros_like(w) for w in params))
    totals, (slot_outs, slot_grads) = lax.scan(one_slot, initial, (stacked_inputs, stacked_cot, stacked_routes, placed_lengths))
    outputs = jnp.take(slot_outs, placement, axis=0).reshape(TOKENS, D)
    input_grad = jnp.take(slot_grads, placement, axis=0).reshape(TOKENS, D)
    return (outputs, input_grad, totals[0], totals[1], totals[2], totals[3], totals[4], totals[5], totals[6], totals[7], totals[8], totals[9])
```

```python
import jax
import jax.numpy as jnp
from jax import lax
from jax.sharding import PartitionSpec as P

HEAD_DIM = 64


EPSILON = 1e-06
ROPE_BASE = 10000.0
PRECISE = lax.Precision.HIGHEST
NEGATIVE = -1e30


def rope_tables(positions, half_dim):
    freq_index = jnp.arange(half_dim, dtype=jnp.int32).astype(jnp.float32)
    frequency = jnp.exp(-(2.0 * freq_index / (2.0 * half_dim)) * jnp.log(ROPE_BASE))
    angles = positions.astype(jnp.float32)[:, None] * frequency[None, :]
    return (jnp.cos(angles)[:, None, :], jnp.sin(angles)[:, None, :])


def rotate(values, cos_table, sin_table):
    half_dim = values.shape[-1] // 2
    first_half = values[..., :half_dim]
    second = values[..., half_dim:]
    return jnp.concatenate(
        [first_half * cos_table - second * sin_table, second * cos_table + first_half * sin_table],
        axis=-1,
    )


def rotate_back(values, cos_table, sin_table):
    half_dim = values.shape[-1] // 2
    first_half = values[..., :half_dim]
    second = values[..., half_dim:]
    return jnp.concatenate(
        [first_half * cos_table + second * sin_table, second * cos_table - first_half * sin_table],
        axis=-1,
    )


def split_parts(values):
    upper = values.astype(jnp.bfloat16)
    lower = (values - upper.astype(jnp.float32)).astype(jnp.bfloat16)
    return (upper, lower)


def swap_tensor(values):
    return lax.ppermute(values, "tensor", [(0, 1), (1, 0)])


def mm(left, right, contract):
    return lax.dot_general(
        left, right, ((contract[:1], contract[1:]), ((), ())), preferred_element_type=jnp.float32
    )


def local(
    inputs,
    cotangent,
    attn_gain,
    expert_gain,
    query_weight,
    key_weight,
    value_weight,
    output_weight,
    router_weight,
    gate_weight,
    up_weight,
    down_weight,
    routes,
    lengths,
    placement,
):
    row_count, top_count = routes.shape
    expert_count = router_weight.shape[1]
    capacity = row_count * top_count // expert_count
    kv_local = key_weight.shape[1] // HEAD_DIM
    heads_local = query_weight.shape[1] // HEAD_DIM
    group = heads_local // kv_local
    scale = 1.0 / HEAD_DIM
    width_half = inputs.shape[1]
    width = 2 * width_half
    plane = lax.axis_index("tensor")
    devices = lax.axis_size("dp")
    dp_index = lax.axis_index("dp")
    plane_experts = expert_count // 2
    members = plane_experts
    clusters = devices // members
    member = dp_index % members
    if clusters == 1:
        inside = across = None
    else:
        inside = [[c * members + m for m in range(members)] for c in range(clusters)]
        across = [[c * members + m for c in range(clusters)] for m in range(members)]

    def exchange(values):
        return lax.all_to_all(
            values, "dp", split_axis=0, concat_axis=0, tiled=True, axis_index_groups=inside
        )

    def gather_small(values):
        return lax.all_gather(values, "dp", axis=0, tiled=False, axis_index_groups=inside)

    def halves(values, axis):
        size = values.shape[axis] // 2
        return (
            lax.dynamic_slice_in_dim(values, plane * size, size, axis),
            lax.dynamic_slice_in_dim(values, (1 - plane) * size, size, axis),
        )

    def join(own, other, axis):
        first = jnp.where(plane == 0, own, other)
        second = jnp.where(plane == 0, other, own)
        return jnp.concatenate([first, second], axis=axis)

    def add_planes(part):
        low = part.astype(jnp.bfloat16)
        return low.astype(jnp.float32) + swap_tensor(low).astype(jnp.float32)

    down_t = jnp.swapaxes(down_weight, 1, 2)
    stacked = jnp.stack([gate_weight, up_weight, down_t], axis=1)
    own_w, other_w = halves(stacked, 0)
    other_w = swap_tensor(other_w)

    def place_weights(values):
        values = exchange(values)
        if clusters > 1:
            values = lax.all_gather(values, "dp", axis=0, tiled=True, axis_index_groups=across)
        return [values[:, i].reshape(width, -1) for i in range(3)]

    own_w = place_weights(own_w)
    other_w = place_weights(other_w)
    gate_full, up_full, down_full = [
        jnp.concatenate([a, b], axis=1) for a, b in zip(own_w, other_w)
    ]

    rank_list = jnp.arange(devices, dtype=jnp.int32)
    holder = jnp.sum(jnp.where(placement == dp_index, rank_list, 0))
    slot_lengths = lax.dynamic_index_in_dim(lengths, holder, 0, keepdims=False)
    seq_count = slot_lengths.shape[0]
    seq_ids = jnp.arange(seq_count, dtype=jnp.int32)
    seg_ends = jnp.sum(
        jnp.where(seq_ids[None, :] <= seq_ids[:, None], slot_lengths[None, :], 0), axis=1
    )
    row_index = jnp.arange(row_count, dtype=jnp.int32)
    past = row_index[:, None] >= seg_ends[None, :]
    segment = jnp.sum(past.astype(jnp.int32), axis=1)
    positions = row_index - jnp.max(jnp.where(past, seg_ends[None, :], 0), axis=1)
    token_live = segment < seq_count
    allowed = (segment[:, None] == segment[None, :]) & (row_index[None, :] <= row_index[:, None])
    cos_table, sin_table = rope_tables(positions, HEAD_DIM // 2)
    live_column = token_live.astype(jnp.float32)[:, None]
    experts = jnp.arange(expert_count, dtype=jnp.int32)
    picked = jnp.any(routes.T[:, None, :] == experts[None, :, None], axis=0)
    counted = picked & token_live[None, :]
    before = (row_index[:, None] < row_index[None, :]).astype(jnp.bfloat16)
    place = mm(counted.astype(jnp.bfloat16), before, (1, 0)).astype(jnp.int32)
    slot_of = jnp.where(counted & (place < capacity), place, -1)
    slot_own = lax.dynamic_slice_in_dim(slot_of, plane * plane_experts, plane_experts, 0)
    hot = slot_own[:, None, :] == jnp.arange(capacity, dtype=jnp.int32)[None, :, None]
    dispatch_t = hot.astype(jnp.bfloat16).reshape(plane_experts * capacity, row_count)

    full_cot = join(cotangent, swap_tensor(cotangent), 1)
    slot_cot = mm(dispatch_t, full_cot, (1, 0)).astype(jnp.bfloat16)
    slot_cot = exchange(slot_cot)

    full_inputs = join(inputs, swap_tensor(inputs), 1)
    wide_inputs = full_inputs.astype(jnp.float32)
    attn_scale = lax.rsqrt(jnp.mean(wide_inputs * wide_inputs, axis=-1, keepdims=True) + EPSILON)
    normed = (wide_inputs * attn_scale * attn_gain).astype(jnp.bfloat16)
    query_pre = jnp.dot(normed, query_weight, preferred_element_type=jnp.float32)
    key_pre = jnp.dot(normed, key_weight, preferred_element_type=jnp.float32)
    value_pre = jnp.dot(normed, value_weight, preferred_element_type=jnp.float32)
    query_rot = (
        rotate(query_pre.reshape(row_count, heads_local, HEAD_DIM), cos_table, sin_table)
        .astype(jnp.bfloat16)
        .reshape(row_count, kv_local, group, HEAD_DIM)
    )
    key_rot = rotate(key_pre.reshape(row_count, kv_local, HEAD_DIM), cos_table, sin_table).astype(
        jnp.bfloat16
    )
    value_rows = value_pre.astype(jnp.bfloat16).reshape(row_count, kv_local, HEAD_DIM)

    def masked_scores():
        raw_scores = (
            jnp.einsum("qhgd,khd->hgqk", query_rot, key_rot, preferred_element_type=jnp.float32)
            * scale
        )
        return jnp.where(allowed, raw_scores, NEGATIVE)

    masked = masked_scores()
    row_max = jnp.max(masked, axis=-1, keepdims=True)
    exp_terms = jnp.exp(masked - row_max)
    row_total = jnp.sum(exp_terms, axis=-1, keepdims=True)
    attn_probs = exp_terms / row_total
    log_total = row_max + jnp.log(row_total)
    context = jnp.einsum(
        "hgqk,khd->qhgd",
        attn_probs.astype(jnp.bfloat16),
        value_rows,
        preferred_element_type=jnp.float32,
    ).reshape(row_count, heads_local * HEAD_DIM)
    context = (context * live_column).astype(jnp.bfloat16)
    attn_part = jnp.dot(context, output_weight, preferred_element_type=jnp.float32)
    residual = wide_inputs + add_planes(attn_part)
    expert_scale = lax.rsqrt(jnp.mean(residual * residual, axis=-1, keepdims=True) + EPSILON)
    mixed_rows = (residual * expert_scale * expert_gain).astype(jnp.bfloat16)

    slot_in = exchange(mm(dispatch_t, mixed_rows, (1, 0)).astype(jnp.bfloat16))

    logits = mm(router_weight, mixed_rows, (0, 1))
    logits = jnp.where(picked, logits, NEGATIVE)
    weights = jnp.exp(logits - jnp.max(logits, axis=0, keepdims=True))
    gates = weights / jnp.sum(weights, axis=0, keepdims=True)
    gates_own = lax.dynamic_slice_in_dim(gates, plane * plane_experts, plane_experts, 0)
    weighted = jnp.where(hot, gates_own[:, None, :], 0.0)
    gate_slot = jnp.sum(weighted, axis=2)
    weighted = weighted.astype(jnp.bfloat16).reshape(plane_experts * capacity, row_count)
    gate_rows = lax.dynamic_index_in_dim(gather_small(gate_slot), member, 1, keepdims=False)
    gate_rows = gate_rows.reshape(members * capacity, 1)

    gate_pre = mm(slot_in, gate_full, (1, 0))
    up_pre = mm(slot_in, up_full, (1, 0))
    sigma = jax.nn.sigmoid(gate_pre)
    hidden = (gate_pre * sigma * up_pre).astype(jnp.bfloat16)
    expert_out = mm(hidden, down_full, (1, 1))
    slot_gate_grad = jnp.sum(expert_out * slot_cot.astype(jnp.float32), axis=1)
    slot_gate_grad = slot_gate_grad.reshape(members, capacity)
    slot_gate_grad = lax.dynamic_index_in_dim(
        gather_small(slot_gate_grad), member, 1, keepdims=False
    )
    hidden_grad = mm(slot_cot, down_full, (1, 0))
    gate_pre_grad = hidden_grad * up_pre * sigma * (1.0 + gate_pre * (1.0 - sigma))
    up_pre_grad = hidden_grad * gate_pre * sigma
    slot_in_grad = mm(gate_pre_grad.astype(jnp.bfloat16), gate_full, (1, 1)) + mm(
        up_pre_grad.astype(jnp.bfloat16), up_full, (1, 1)
    )
    slot_in_grad = exchange(slot_in_grad.astype(jnp.bfloat16))
    expert_out = exchange(expert_out.astype(jnp.bfloat16))
    scaled_cot = (gate_rows * slot_cot.astype(jnp.float32)).astype(jnp.bfloat16)
    w_grads = [
        mm(slot_in, (gate_rows * gate_pre_grad).astype(jnp.bfloat16), (0, 0)),
        mm(slot_in, (gate_rows * up_pre_grad).astype(jnp.bfloat16), (0, 0)),
        mm(scaled_cot, hidden, (0, 0)),
    ]
    w_grads = jnp.stack([w.reshape(devices, width // devices, -1) for w in w_grads], axis=1)
    w_grads = w_grads.astype(jnp.bfloat16)

    moe_part = mm(weighted, expert_out, (0, 0)).astype(jnp.bfloat16)
    moe_own, moe_other = halves(moe_part, 1)
    moe_half = moe_own.astype(jnp.float32) + swap_tensor(moe_other).astype(jnp.float32)
    residual_half, _ = halves(residual, 1)
    outputs_half = (residual_half + moe_half).astype(jnp.bfloat16)

    token_gate_grad = jnp.sum(
        jnp.where(hot, slot_gate_grad[:, :, None], 0.0), axis=1
    )
    mean_grad = jnp.sum(gates_own * token_gate_grad, axis=0, keepdims=True)
    spread = jnp.zeros_like(gates)
    spread = lax.dynamic_update_slice_in_dim(spread, token_gate_grad, plane * plane_experts, 0)
    logits_grad = gates * (spread - mean_grad)
    logits_upper, logits_lower = split_parts(logits_grad)
    router_part = mm(logits_upper, mixed_rows, (1, 0)) + mm(logits_lower, mixed_rows, (1, 0))
    router_grad = add_planes(router_part)
    mixed_part = (
        mm(weighted, slot_in_grad, (0, 0))
        + mm(logits_upper, router_weight, (0, 1))
        + mm(logits_lower, router_weight, (0, 1))
    )
    mixed_grad = add_planes(mixed_part)
    scaled_two = mixed_grad * expert_gain
    expert_gain_grad = jnp.sum(mixed_grad * residual * expert_scale, axis=0)
    cube_two = expert_scale * expert_scale * expert_scale
    residual_grad = (
        full_cot.astype(jnp.float32)
        + expert_scale * scaled_two
        - residual * cube_two * jnp.mean(scaled_two * residual, axis=-1, keepdims=True)
    )
    residual_low = residual_grad.astype(jnp.bfloat16)
    output_w_grad = mm(residual_low, context, (0, 0))
    context_grad = jnp.einsum(
        "td,hd->th", residual_low, output_weight, preferred_element_type=jnp.float32
    ).astype(jnp.bfloat16)
    context_grad = jnp.where(
        token_live[:, None], context_grad, jnp.zeros_like(context_grad)
    ).reshape(row_count, kv_local, group, HEAD_DIM)
    again = masked_scores()
    probs_again = jnp.exp(again - log_total)
    prob_grad = jnp.einsum(
        "qhgd,khd->hgqk", context_grad, value_rows, preferred_element_type=jnp.float32
    )
    row_inner = jnp.sum(probs_again * prob_grad, axis=-1, keepdims=True)
    score_grad = (probs_again * (prob_grad - row_inner)).astype(jnp.bfloat16)
    query_grad = (
        jnp.einsum("hgqk,khd->qhgd", score_grad, key_rot, preferred_element_type=jnp.float32)
        * scale
    )
    key_grad = (
        jnp.einsum("hgqk,qhgd->khd", score_grad, query_rot, preferred_element_type=jnp.float32)
        * scale
    )
    value_grad = jnp.einsum(
        "hgqk,qhgd->khd",
        probs_again.astype(jnp.bfloat16),
        context_grad,
        preferred_element_type=jnp.float32,
    )
    query_pre_grad = (
        rotate_back(query_grad.reshape(row_count, heads_local, HEAD_DIM), cos_table, sin_table)
        .astype(jnp.bfloat16)
        .reshape(row_count, -1)
    )
    key_pre_grad = (
        rotate_back(key_grad, cos_table, sin_table).astype(jnp.bfloat16).reshape(row_count, -1)
    )
    value_pre_grad = value_grad.astype(jnp.bfloat16).reshape(row_count, -1)
    query_w_grad = mm(normed, query_pre_grad, (0, 0))
    key_w_grad = mm(normed, key_pre_grad, (0, 0))
    value_w_grad = mm(normed, value_pre_grad, (0, 0))
    normed_part = (
        mm(query_pre_grad, query_weight, (1, 1))
        + mm(key_pre_grad, key_weight, (1, 1))
        + mm(value_pre_grad, value_weight, (1, 1))
    )
    normed_grad = add_planes(normed_part)
    scaled_one = normed_grad * attn_gain
    attn_gain_grad = jnp.sum(normed_grad * wide_inputs * attn_scale, axis=0)
    cube_one = attn_scale * attn_scale * attn_scale
    input_grad = (
        residual_grad
        + attn_scale * scaled_one
        - wide_inputs * cube_one * jnp.mean(scaled_one * wide_inputs, axis=-1, keepdims=True)
    )
    input_half, _ = halves(input_grad, 1)

    vectors = jnp.concatenate(
        [router_grad, attn_gain_grad[None], expert_gain_grad[None]], axis=0
    ).T
    vectors = jnp.pad(vectors, ((0, 0), (0, 128 - vectors.shape[1])))
    parts = jnp.concatenate(
        [output_w_grad, query_w_grad, key_w_grad, value_w_grad, vectors], axis=1
    ).astype(jnp.bfloat16)
    share = lax.psum_scatter(parts, "dp", scatter_dimension=0, tiled=True).astype(jnp.float32)
    cuts = [output_w_grad.shape[1]]
    for w in (query_w_grad, key_w_grad, value_w_grad):
        cuts.append(cuts[-1] + w.shape[1])
    output_part = share[:, : cuts[0]].T
    query_part = share[:, cuts[0] : cuts[1]]
    key_part = share[:, cuts[1] : cuts[2]]
    value_part = share[:, cuts[2] : cuts[3]]
    router_share = share[:, cuts[3] : cuts[3] + expert_count]
    attn_gain_part = share[:, cuts[3] + expert_count]
    expert_gain_part = share[:, cuts[3] + expert_count + 1]

    own_g, other_g = jnp.split(w_grads, 2, axis=3)

    def return_grads(values):
        if clusters > 1:
            values = lax.psum_scatter(
                values, "dp", scatter_dimension=0, tiled=True, axis_index_groups=across
            )
        return exchange(values)

    other_g = swap_tensor(return_grads(other_g))
    own_g = return_grads(own_g)
    both = join(own_g, other_g, 0).astype(jnp.float32)
    gate_w_part = both[:, 0]
    up_w_part = both[:, 1]
    down_w_part = jnp.swapaxes(both[:, 2], 1, 2)

    piece_rows = row_count // devices

    def reroute(values):
        spread = lax.all_to_all(
            values.reshape(devices, piece_rows, -1), "dp", split_axis=0, concat_axis=0, tiled=True
        )
        moved = jnp.take(spread, placement, axis=0)
        return lax.all_to_all(moved, "dp", split_axis=0, concat_axis=0, tiled=True).reshape(
            row_count, -1
        )

    outputs = reroute(outputs_half)
    input_result = reroute(input_half.astype(jnp.bfloat16)).astype(jnp.float32)
    return (
        outputs,
        input_result,
        attn_gain_part,
        expert_gain_part,
        query_part,
        key_part,
        value_part,
        output_part,
        router_share,
        gate_w_part,
        up_w_part,
        down_w_part,
    )


def solution(mesh):
    in_specs = (
        P("dp", "tensor"),
        P("dp", "tensor"),
        P(),
        P(),
        P(None, "tensor"),
        P(None, "tensor"),
        P(None, "tensor"),
        P("tensor", None),
        P(),
        P(None, "dp", "tensor"),
        P(None, "dp", "tensor"),
        P(None, "tensor", "dp"),
        P("dp", None),
        P(),
        P(),
    )
    out_specs = (
        P("dp", "tensor"),
        P("dp", "tensor"),
        P("dp"),
        P("dp"),
        P("dp", "tensor"),
        P("dp", "tensor"),
        P("dp", "tensor"),
        P("tensor", "dp"),
        P("dp", None),
        P(None, "dp", "tensor"),
        P(None, "dp", "tensor"),
        P(None, "tensor", "dp"),
    )
    return jax.shard_map(local, mesh=mesh, in_specs=in_specs, out_specs=out_specs, check_vma=False)
```

```python
import jax
import jax.numpy as jnp
from jax import lax
from jax.experimental import pallas as pl
from jax.experimental.pallas import tpu as pltpu
from jax.sharding import PartitionSpec as P

HEAD_DIM = 64


EPSILON = 1e-06
ROPE_BASE = 10000.0
PRECISE = lax.Precision.HIGHEST
NEGATIVE = -1e30


def rope_tables(positions, half_dim):
    freq_index = jnp.arange(half_dim, dtype=jnp.int32).astype(jnp.float32)
    frequency = jnp.exp(-(2.0 * freq_index / (2.0 * half_dim)) * jnp.log(ROPE_BASE))
    angles = positions.astype(jnp.float32)[:, None] * frequency[None, :]
    return (jnp.cos(angles)[:, None, :], jnp.sin(angles)[:, None, :])


def rotate(values, cos_table, sin_table):
    half_dim = values.shape[-1] // 2
    first_half = values[..., :half_dim]
    second = values[..., half_dim:]
    return jnp.concatenate(
        [first_half * cos_table - second * sin_table, second * cos_table + first_half * sin_table],
        axis=-1,
    )


def rotate_back(values, cos_table, sin_table):
    half_dim = values.shape[-1] // 2
    first_half = values[..., :half_dim]
    second = values[..., half_dim:]
    return jnp.concatenate(
        [first_half * cos_table + second * sin_table, second * cos_table - first_half * sin_table],
        axis=-1,
    )


def split_parts(values):
    upper = values.astype(jnp.bfloat16)
    lower = (values - upper.astype(jnp.float32)).astype(jnp.bfloat16)
    return (upper, lower)


def swap_tensor(values):
    return lax.ppermute(values, "tensor", [(0, 1), (1, 0)])


def mm(left, right, contract):
    return lax.dot_general(
        left, right, ((contract[:1], contract[1:]), ((), ())), preferred_element_type=jnp.float32
    )


def after(values, *others):
    return lax.optimization_barrier((values,) + others)[0]


def dot(left, right, left_axis=1, right_axis=0):
    return lax.dot_general(
        left,
        right,
        (((left_axis,), (right_axis,)), ((), ())),
        preferred_element_type=jnp.float32,
    )


def expert_kernel(
    expert_ref,
    rows_ref,
    cot_ref,
    gate_ref,
    pair_ref,
    router_ref,
    back_ref,
    moe_ref,
    hidden_ref,
    gate_grad_ref,
    up_grad_ref,
    slot_grad_ref,
    logits_ref,
):
    width = rows_ref.shape[1]
    expert_count = router_ref.shape[0]
    rows = rows_ref[...]
    cot = cot_ref[:, :width].astype(jnp.float32)
    router = router_ref[...]
    logits = jnp.where(
        cot_ref[:, width : width + expert_count].astype(jnp.float32) > 0.5,
        dot(rows, router, 1, 1),
        NEGATIVE,
    )
    terms = jnp.exp(logits - jnp.max(logits, axis=1, keepdims=True))
    gates = terms / jnp.sum(terms, axis=1, keepdims=True)
    own = (lax.broadcasted_iota(jnp.int32, gates.shape, 1) == expert_ref[0]).astype(jnp.float32)
    gate = jnp.sum(gates * own, axis=1, keepdims=True)

    def weight(ref, *place):
        value = ref[(slice(None),) + place]
        return value.reshape(width, value.shape[-1])

    halves = range(gate_ref.shape[1])
    columns = gate_ref.shape[-1]
    kept = []
    out = 0.0
    for f in halves:
        gate_pre = dot(rows, weight(gate_ref, f))
        up_pre = dot(rows, weight(pair_ref, f, 0))
        sigma = 1.0 / (1.0 + jnp.exp(-gate_pre))
        hidden = (gate_pre * sigma * up_pre).astype(jnp.bfloat16)
        hidden_ref[:, f * columns : (f + 1) * columns] = hidden
        out = out + dot(hidden, weight(pair_ref, f, 1), 1, 1)
        kept.append((gate_pre, up_pre, sigma))
    gate_grad = jnp.sum(out * cot, axis=1, keepdims=True)
    moe_ref[...] = (gate * out).astype(jnp.bfloat16)
    slot_grad = (gate * cot).astype(jnp.bfloat16)
    slot_grad_ref[...] = slot_grad
    logits_grad = gate_grad * gate * (own - gates)
    upper = logits_grad.astype(jnp.bfloat16)
    lower = (logits_grad - upper.astype(jnp.float32)).astype(jnp.bfloat16)
    logits_ref[0] = upper
    logits_ref[1] = lower
    back = dot(upper, router) + dot(lower, router)
    for f in halves:
        gate_pre, up_pre, sigma = kept[f]
        hidden_grad = dot(slot_grad, weight(pair_ref, f, 1))
        gate_pre_grad = hidden_grad * up_pre * sigma * (1.0 + gate_pre * (1.0 - sigma))
        gate_pre_grad = gate_pre_grad.astype(jnp.bfloat16)
        up_pre_grad = (hidden_grad * gate_pre * sigma).astype(jnp.bfloat16)
        gate_grad_ref[:, f * columns : (f + 1) * columns] = gate_pre_grad
        up_grad_ref[:, f * columns : (f + 1) * columns] = up_pre_grad
        back = back + dot(gate_pre_grad, weight(gate_ref, f), 1, 1)
        back = back + dot(up_pre_grad, weight(pair_ref, f, 0), 1, 1)
    back_ref[...] = back.astype(jnp.bfloat16)


def run_expert(expert, rows, cot, gate_w, pair_w, router_t):
    count, width = rows.shape
    hidden = 2 * gate_w.shape[-1]
    step = count // 4
    bf16 = jnp.bfloat16
    row_block = lambda columns: pl.BlockSpec((step, columns), lambda i: (i, 0))
    whole = lambda value: pl.BlockSpec(value.shape, lambda i: (0,) * value.ndim)
    experts = router_t.shape[0]
    return pl.pallas_call(
        expert_kernel,
        grid=(4,),
        in_specs=[
            pl.BlockSpec(memory_space=pltpu.SMEM),
            row_block(width),
            row_block(cot.shape[1]),
            whole(gate_w),
            whole(pair_w),
            whole(router_t),
        ],
        out_specs=[
            row_block(width),
            row_block(width),
            row_block(hidden),
            row_block(hidden),
            row_block(hidden),
            row_block(width),
            pl.BlockSpec((2, step, experts), lambda i: (0, i, 0)),
        ],
        out_shape=[
            jax.ShapeDtypeStruct((count, width), bf16),
            jax.ShapeDtypeStruct((count, width), bf16),
            jax.ShapeDtypeStruct((count, hidden), bf16),
            jax.ShapeDtypeStruct((count, hidden), bf16),
            jax.ShapeDtypeStruct((count, hidden), bf16),
            jax.ShapeDtypeStruct((count, width), bf16),
            jax.ShapeDtypeStruct((2, count, experts), bf16),
        ],
        compiler_params=pltpu.CompilerParams(vmem_limit_bytes=48 << 20),
        cost_estimate=pl.CostEstimate(
            flops=12 * count * width * hidden, bytes_accessed=16 << 20, transcendentals=count * hidden
        ),
        name="expert_rows",
    )(expert.reshape(1), rows, cot, gate_w, pair_w, router_t)


def expert_grad_kernel(
    rows_ref, slot_grad_ref, hidden_ref, gate_grad_ref, up_grad_ref, logits_ref, out_ref, router_ref
):
    rows = rows_ref[...]
    blocks, planes, _, block_rows, columns = out_ref.shape
    pieces = (
        dot(rows, gate_grad_ref[...], 0, 0),
        dot(rows, up_grad_ref[...], 0, 0),
        dot(slot_grad_ref[...], hidden_ref[...], 0, 0),
    )
    for i, piece in enumerate(pieces):
        piece = piece.astype(jnp.bfloat16)
        for f in range(planes):
            out_ref[:, f, i] = piece[:, f * columns : (f + 1) * columns].reshape(
                blocks, block_rows, columns
            )
    router_ref[...] = dot(logits_ref[0], rows, 0, 0) + dot(logits_ref[1], rows, 0, 0)


def run_expert_grads(rows, slot_grad, hidden, gate_grad, up_grad, logits, shape):
    count, width = rows.shape
    steps = 4
    step = width // steps
    blocks = shape[0] // steps
    column_block = pl.BlockSpec((count, step), lambda i: (0, i))
    whole = lambda value: pl.BlockSpec(value.shape, lambda i: (0,) * value.ndim)
    experts = logits.shape[2]
    return pl.pallas_call(
        expert_grad_kernel,
        grid=(steps,),
        in_specs=[
            column_block,
            column_block,
            whole(hidden),
            whole(gate_grad),
            whole(up_grad),
            whole(logits),
        ],
        out_specs=[
            pl.BlockSpec((blocks,) + shape[1:], lambda i: (i, 0, 0, 0, 0)),
            pl.BlockSpec((experts, step), lambda i: (0, i)),
        ],
        out_shape=[
            jax.ShapeDtypeStruct(shape, jnp.bfloat16),
            jax.ShapeDtypeStruct((experts, width), jnp.float32),
        ],
        compiler_params=pltpu.CompilerParams(vmem_limit_bytes=48 << 20),
        cost_estimate=pl.CostEstimate(
            flops=6 * count * width * hidden.shape[1], bytes_accessed=12 << 20, transcendentals=0
        ),
        name="expert_grads",
    )(rows, slot_grad, hidden, gate_grad, up_grad, logits)


def local(
    inputs,
    cotangent,
    attn_gain,
    expert_gain,
    query_weight,
    key_weight,
    value_weight,
    output_weight,
    router_weight,
    gate_weight,
    up_weight,
    down_weight,
    routes,
    lengths,
    placement,
):
    row_count, top_count = routes.shape
    expert_count = router_weight.shape[1]
    capacity = row_count * top_count // expert_count
    kv_local = key_weight.shape[1] // HEAD_DIM
    heads_local = query_weight.shape[1] // HEAD_DIM
    group = heads_local // kv_local
    scale = 1.0 / HEAD_DIM
    width_half = inputs.shape[1]
    width = 2 * width_half
    plane = lax.axis_index("tensor")
    devices = lax.axis_size("dp")
    dp_index = lax.axis_index("dp")
    members = expert_count // 2
    near = members // 2
    clusters = devices // members
    member = dp_index % members
    expert = 2 * member + plane
    inside = [[c * members + m for m in range(members)] for c in range(clusters)]
    across = [[c * members + m for c in range(clusters)] for m in range(members)]

    def cross(values):
        return lax.ppermute(values, "dp", [(i, i ^ near) for i in range(devices)])

    def spread(blocks):
        return [blocks[0]] + [
            lax.ppermute(blocks[s], "dp", [(i, i ^ s) for i in range(devices)])
            for s in range(1, near)
        ]

    def halves(values, axis):
        size = values.shape[axis] // 2
        return (
            lax.dynamic_slice_in_dim(values, plane * size, size, axis),
            lax.dynamic_slice_in_dim(values, (1 - plane) * size, size, axis),
        )

    def join(own, other, axis):
        first = jnp.where(plane == 0, own, other)
        second = jnp.where(plane == 0, other, own)
        return jnp.concatenate([first, second], axis=axis)

    def add_planes(part):
        low = part.astype(jnp.bfloat16)
        return low.astype(jnp.float32) + swap_tensor(low).astype(jnp.float32)

    routes_t = routes.T
    routes_pair = jnp.stack([routes_t, cross(routes_t)])
    full_inputs = join(inputs, swap_tensor(inputs), 1)
    cot_cross = cross(cotangent)

    def to_owner(values):
        if clusters == 1:
            owned = lax.all_to_all(
                values, ("dp", "tensor"), split_axis=0, concat_axis=0, tiled=True
            )
            return owned.reshape((devices, 2) + owned.shape[1:])
        by_plane = values.reshape((members, 2) + values.shape[1:])
        own_w = lax.dynamic_index_in_dim(by_plane, plane, 1, keepdims=False)
        other_w = swap_tensor(lax.dynamic_index_in_dim(by_plane, 1 - plane, 1, keepdims=False))
        owned = jnp.stack(
            [jnp.where(plane == 0, own_w, other_w), jnp.where(plane == 0, other_w, own_w)], axis=1
        )
        owned = lax.all_to_all(
            owned, "dp", split_axis=0, concat_axis=0, tiled=True, axis_index_groups=inside
        )
        owned = lax.all_gather(owned, "dp", axis=0, tiled=True, axis_index_groups=across)
        owned = owned.reshape((members, clusters) + owned.shape[1:])
        owned = jnp.moveaxis(owned, 1, -3)
        return owned.reshape(owned.shape[:-3] + (-1, owned.shape[-1]))

    def from_owner(values):
        if clusters == 1:
            return lax.all_to_all(
                values.reshape((2 * devices,) + values.shape[2:]),
                ("dp", "tensor"),
                split_axis=0,
                concat_axis=0,
                tiled=True,
            )
        values = values.reshape(values.shape[:-2] + (clusters, -1, values.shape[-1]))
        values = jnp.moveaxis(values, -3, 1)
        values = values.reshape((devices,) + values.shape[2:])
        values = lax.psum_scatter(
            values, "dp", scatter_dimension=0, tiled=True, axis_index_groups=across
        )
        values = lax.all_to_all(
            values, "dp", split_axis=0, concat_axis=0, tiled=True, axis_index_groups=inside
        )
        own_g = lax.dynamic_index_in_dim(values, plane, 1, keepdims=False)
        other_g = swap_tensor(lax.dynamic_index_in_dim(values, 1 - plane, 1, keepdims=False))
        values = jnp.stack(
            [jnp.where(plane == 0, own_g, other_g), jnp.where(plane == 0, other_g, own_g)], axis=1
        )
        return values.reshape((expert_count,) + values.shape[2:])

    owned_gate = to_owner(after(gate_weight, cot_cross))

    cot_pair = jnp.concatenate([cotangent, cot_cross], axis=0)
    cot_pair = join(cot_pair, swap_tensor(cot_pair), 1)
    full_cot = cot_pair[:row_count]

    rank_list = jnp.arange(devices, dtype=jnp.int32)
    holder = jnp.sum(jnp.where(placement == dp_index, rank_list, 0))
    slot_lengths = lax.dynamic_index_in_dim(lengths, holder, 0, keepdims=False)
    seq_count = slot_lengths.shape[0]
    seq_ids = jnp.arange(seq_count, dtype=jnp.int32)
    seg_ends = jnp.sum(
        jnp.where(seq_ids[None, :] <= seq_ids[:, None], slot_lengths[None, :], 0), axis=1
    )
    row_index = jnp.arange(row_count, dtype=jnp.int32)
    past = row_index[:, None] >= seg_ends[None, :]
    segment = jnp.sum(past.astype(jnp.int32), axis=1)
    positions = row_index - jnp.max(jnp.where(past, seg_ends[None, :], 0), axis=1)
    token_live = row_index < jnp.sum(slot_lengths)
    allowed = (segment[:, None] == segment[None, :]) & (row_index[None, :] <= row_index[:, None])
    cos_table, sin_table = rope_tables(positions, HEAD_DIM // 2)
    live_column = token_live.astype(jnp.float32)[:, None]

    before = (row_index[:, None] < row_index[None, :]).astype(jnp.bfloat16)
    experts = jnp.arange(expert_count, dtype=jnp.int32)
    near_ids = jnp.arange(near, dtype=jnp.int32)
    near_experts = 2 * (member ^ near_ids) + plane
    counted = jnp.any(routes_pair[None] == near_experts[:, None, None, None], axis=2)
    counted = (counted & token_live[None, None, :]).reshape(2 * near, row_count)
    place = mm(counted.astype(jnp.bfloat16), before, (1, 0)).astype(jnp.int32)
    place = jnp.where(counted & (place < capacity), place, -1).reshape(near, 2, 1, 1, row_count)
    pair_ids = jnp.arange(2, dtype=jnp.int32)
    same = pair_ids[:, None] == pair_ids[None, :]
    slots = jnp.arange(capacity, dtype=jnp.int32)
    hot = (place == slots[None, None, :, None, None]) & same[None, :, None, :, None]
    hot = hot.astype(jnp.bfloat16).reshape(2 * near * capacity, 2 * row_count)
    picked = jnp.any(routes_pair[:, :, :, None] == experts[None, None, None, :], axis=1)
    picked = jnp.pad(
        picked.astype(jnp.bfloat16).reshape(2 * row_count, expert_count),
        ((0, 0), (0, 128 - expert_count)),
    )

    def dispatch(tokens):
        rows = mm(hot, tokens, (1, 0)).astype(jnp.bfloat16)
        return jnp.concatenate(spread(jnp.split(rows, near, axis=0)), axis=0)

    def combine(rows):
        rows = jnp.concatenate(spread(jnp.split(rows, near, axis=0)), axis=0)
        parts = mm(hot, rows, (0, 0))
        mine, others = parts[:row_count], parts[row_count:]
        others_own, others_away = halves(others, 1)
        mine_own, mine_away = halves(mine, 1)
        others = others_own + swap_tensor(others_away.astype(jnp.bfloat16)).astype(jnp.float32)
        mine = mine_own + swap_tensor(mine_away.astype(jnp.bfloat16)).astype(jnp.float32)
        return mine + cross(others.astype(jnp.bfloat16)).astype(jnp.float32)

    slot_cot = dispatch(jnp.concatenate([cot_pair, picked], axis=1))

    wide_inputs = full_inputs.astype(jnp.float32)
    attn_scale = lax.rsqrt(jnp.mean(wide_inputs * wide_inputs, axis=-1, keepdims=True) + EPSILON)
    normed = (wide_inputs * attn_scale * attn_gain).astype(jnp.bfloat16)
    query_pre = jnp.dot(normed, query_weight, preferred_element_type=jnp.float32)
    key_pre = jnp.dot(normed, key_weight, preferred_element_type=jnp.float32)
    value_pre = jnp.dot(normed, value_weight, preferred_element_type=jnp.float32)
    query_rot = (
        rotate(query_pre.reshape(row_count, heads_local, HEAD_DIM), cos_table, sin_table)
        .astype(jnp.bfloat16)
        .reshape(row_count, kv_local, group, HEAD_DIM)
    )
    key_rot = rotate(key_pre.reshape(row_count, kv_local, HEAD_DIM), cos_table, sin_table).astype(
        jnp.bfloat16
    )
    value_rows = value_pre.astype(jnp.bfloat16).reshape(row_count, kv_local, HEAD_DIM)

    def masked_scores():
        raw_scores = (
            jnp.einsum("qhgd,khd->hgqk", query_rot, key_rot, preferred_element_type=jnp.float32)
            * scale
        )
        return jnp.where(allowed, raw_scores, NEGATIVE)

    masked = masked_scores()
    row_max = jnp.max(masked, axis=-1, keepdims=True)
    exp_terms = jnp.exp(masked - row_max)
    row_total = jnp.sum(exp_terms, axis=-1, keepdims=True)
    attn_probs = exp_terms / row_total
    log_total = row_max + jnp.log(row_total)
    context = jnp.einsum(
        "hgqk,khd->qhgd",
        attn_probs.astype(jnp.bfloat16),
        value_rows,
        preferred_element_type=jnp.float32,
    ).reshape(row_count, heads_local * HEAD_DIM)
    context = (context * live_column).astype(jnp.bfloat16)
    attn_part = jnp.dot(context, output_weight, preferred_element_type=jnp.float32)
    attn_whole = add_planes(attn_part)
    residual = wide_inputs + attn_whole
    expert_scale = lax.rsqrt(jnp.mean(residual * residual, axis=-1, keepdims=True) + EPSILON)
    mixed_rows = (residual * expert_scale * expert_gain).astype(jnp.bfloat16)
    mixed_cross = cross(halves(mixed_rows, 1)[0])
    owned_pair = to_owner(
        after(jnp.stack([up_weight, jnp.swapaxes(down_weight, 1, 2)], axis=1), mixed_cross)
    )
    mixed_cross = join(mixed_cross, swap_tensor(mixed_cross), 1)
    slot_in = dispatch(jnp.concatenate([mixed_rows, mixed_cross], axis=0))

    slot_back, slot_moe, hidden, gate_pre_grad, up_pre_grad, slot_grad, logits_grad = run_expert(
        expert, slot_in, slot_cot, owned_gate, owned_pair, router_weight.T
    )
    mixed_half = combine(slot_back).astype(jnp.bfloat16)
    w_grads, router_part = run_expert_grads(
        slot_in,
        slot_grad,
        hidden,
        gate_pre_grad,
        up_pre_grad,
        logits_grad,
        (members, 2, 3, width // members, gate_weight.shape[2]),
    )
    mixed_grad = join(mixed_half, after(swap_tensor(mixed_half), w_grads), 1).astype(jnp.float32)
    moe_half = combine(slot_moe)
    outputs_half = (halves(residual, 1)[0] + moe_half).astype(jnp.bfloat16)
    router_grad = add_planes(router_part)

    scaled_two = mixed_grad * expert_gain
    expert_gain_grad = jnp.sum(mixed_grad * residual * expert_scale, axis=0)
    cube_two = expert_scale * expert_scale * expert_scale
    residual_grad = (
        full_cot.astype(jnp.float32)
        + expert_scale * scaled_two
        - residual * cube_two * jnp.mean(scaled_two * residual, axis=-1, keepdims=True)
    )
    residual_low = residual_grad.astype(jnp.bfloat16)
    output_w_grad = mm(residual_low, context, (0, 0))
    context_grad = jnp.einsum(
        "td,hd->th", residual_low, output_weight, preferred_element_type=jnp.float32
    ).astype(jnp.bfloat16)
    context_grad = jnp.where(
        token_live[:, None], context_grad, jnp.zeros_like(context_grad)
    ).reshape(row_count, kv_local, group, HEAD_DIM)
    again = masked_scores()
    probs_again = jnp.exp(again - log_total)
    prob_grad = jnp.einsum(
        "qhgd,khd->hgqk", context_grad, value_rows, preferred_element_type=jnp.float32
    )
    row_inner = jnp.sum(probs_again * prob_grad, axis=-1, keepdims=True)
    score_grad = (probs_again * (prob_grad - row_inner)).astype(jnp.bfloat16)
    query_grad = (
        jnp.einsum("hgqk,khd->qhgd", score_grad, key_rot, preferred_element_type=jnp.float32)
        * scale
    )
    key_grad = (
        jnp.einsum("hgqk,qhgd->khd", score_grad, query_rot, preferred_element_type=jnp.float32)
        * scale
    )
    value_grad = jnp.einsum(
        "hgqk,qhgd->khd",
        probs_again.astype(jnp.bfloat16),
        context_grad,
        preferred_element_type=jnp.float32,
    )
    query_pre_grad = (
        rotate_back(query_grad.reshape(row_count, heads_local, HEAD_DIM), cos_table, sin_table)
        .astype(jnp.bfloat16)
        .reshape(row_count, -1)
    )
    key_pre_grad = (
        rotate_back(key_grad, cos_table, sin_table).astype(jnp.bfloat16).reshape(row_count, -1)
    )
    value_pre_grad = value_grad.astype(jnp.bfloat16).reshape(row_count, -1)
    query_w_grad = mm(normed, query_pre_grad, (0, 0))
    key_w_grad = mm(normed, key_pre_grad, (0, 0))
    value_w_grad = mm(normed, value_pre_grad, (0, 0))
    normed_part = (
        mm(query_pre_grad, query_weight, (1, 1))
        + mm(key_pre_grad, key_weight, (1, 1))
        + mm(value_pre_grad, value_weight, (1, 1))
    )
    normed_grad = add_planes(normed_part)
    scaled_one = normed_grad * attn_gain
    attn_gain_grad = jnp.sum(normed_grad * wide_inputs * attn_scale, axis=0)
    cube_one = attn_scale * attn_scale * attn_scale
    input_grad = (
        residual_grad
        + attn_scale * scaled_one
        - wide_inputs * cube_one * jnp.mean(scaled_one * wide_inputs, axis=-1, keepdims=True)
    )
    input_half, _ = halves(input_grad, 1)

    vectors = jnp.concatenate(
        [router_grad, attn_gain_grad[None], expert_gain_grad[None]], axis=0
    ).T
    vectors = jnp.pad(vectors, ((0, 0), (0, 128 - vectors.shape[1])))
    parts = jnp.concatenate(
        [output_w_grad, query_w_grad, key_w_grad, value_w_grad, vectors], axis=1
    ).astype(jnp.bfloat16)
    share = lax.psum_scatter(parts, "dp", scatter_dimension=0, tiled=True).astype(jnp.float32)
    cuts = [output_w_grad.shape[1]]
    for w in (query_w_grad, key_w_grad, value_w_grad):
        cuts.append(cuts[-1] + w.shape[1])
    output_part = share[:, : cuts[0]].T
    query_part = share[:, cuts[0] : cuts[1]]
    key_part = share[:, cuts[1] : cuts[2]]
    value_part = share[:, cuts[2] : cuts[3]]
    router_share = share[:, cuts[3] : cuts[3] + expert_count]
    attn_gain_part = share[:, cuts[3] + expert_count]
    expert_gain_part = share[:, cuts[3] + expert_count + 1]

    both = from_owner(after(w_grads, mixed_half))
    gate_w_part = both[:, 0].astype(jnp.float32)
    up_w_part = both[:, 1].astype(jnp.float32)
    down_w_part = jnp.swapaxes(both[:, 2], 1, 2).astype(jnp.float32)

    piece_rows = row_count // devices
    moved = jnp.concatenate([outputs_half, input_half.astype(jnp.bfloat16)], axis=1)
    moved = after(moved, both)
    moved = lax.all_to_all(
        moved.reshape(devices, piece_rows, width), "dp", split_axis=0, concat_axis=0, tiled=True
    )
    moved = jnp.take(moved, placement, axis=0)
    moved = lax.all_to_all(moved, "dp", split_axis=0, concat_axis=0, tiled=True)
    moved = moved.reshape(row_count, width)
    outputs = moved[:, :width_half]
    input_result = moved[:, width_half:].astype(jnp.float32)
    return (
        outputs,
        input_result,
        attn_gain_part,
        expert_gain_part,
        query_part,
        key_part,
        value_part,
        output_part,
        router_share,
        gate_w_part,
        up_w_part,
        down_w_part,
    )


def solution(mesh):
    in_specs = (
        P("dp", "tensor"),
        P("dp", "tensor"),
        P(),
        P(),
        P(None, "tensor"),
        P(None, "tensor"),
        P(None, "tensor"),
        P("tensor", None),
        P(),
        P(None, "dp", "tensor"),
        P(None, "dp", "tensor"),
        P(None, "tensor", "dp"),
        P("dp", None),
        P(),
        P(),
    )
    out_specs = (
        P("dp", "tensor"),
        P("dp", "tensor"),
        P("dp"),
        P("dp"),
        P("dp", "tensor"),
        P("dp", "tensor"),
        P("dp", "tensor"),
        P("tensor", "dp"),
        P("dp", None),
        P(None, "dp", "tensor"),
        P(None, "dp", "tensor"),
        P(None, "tensor", "dp"),
    )
    return jax.shard_map(local, mesh=mesh, in_specs=in_specs, out_specs=out_specs, check_vma=False)
```

```python
import functools
import math

import jax
import jax.numpy as jnp
from jax import lax
from jax.experimental import pallas as pl
from jax.experimental.pallas import tpu as pltpu
from jax.sharding import PartitionSpec as P

HEAD_DIM = 64


EPSILON = 1e-06
ROPE_BASE = 10000.0
NEGATIVE = -1e30


def swap_tensor(values):
    return lax.ppermute(values, "tensor", [(0, 1), (1, 0)])


def mm(left, right, contract):
    return lax.dot_general(
        left, right, ((contract[:1], contract[1:]), ((), ())), preferred_element_type=jnp.float32
    )


def after(values, *others):
    return lax.optimization_barrier((values,) + others)[0]


def dot(left, right, left_axis=1, right_axis=0):
    return lax.dot_general(
        left,
        right,
        (((left_axis,), (right_axis,)), ((), ())),
        preferred_element_type=jnp.float32,
    )


def params(megabytes):
    return pltpu.CompilerParams(vmem_limit_bytes=megabytes << 20)


def cost(flops, size, transcendentals=0):
    return pl.CostEstimate(
        flops=flops, bytes_accessed=size, transcendentals=transcendentals
    )


SMEM = pl.BlockSpec(memory_space=pltpu.SMEM)
VMEM = pl.BlockSpec(memory_space=pltpu.VMEM)
ANY = pl.BlockSpec(memory_space=pl.ANY)
FULL = 60


def columns_of(plane, width, own):
    half = width // 2
    start = plane * half if own else (1 - plane) * half
    return pl.ds(pl.multiple_of(start, half), half)


def write_blocks(product, columns, out_refs, capacity, which):
    for j, out_ref in enumerate(out_refs):
        out_ref[which * capacity : (which + 1) * capacity, columns] = product[
            j * capacity : (j + 1) * capacity
        ].astype(out_ref.dtype)


def dispatch_cot_kernel(capacity, expert_count, facts_ref, routes_ref, partner_ref, *refs):
    own_ref, cross_ref, away_ref, cross_away_ref, hot_ref = refs[:5]
    out_refs = refs[5:]
    plane, member, live_count = facts_ref[0], facts_ref[1], facts_ref[2]
    tokens = routes_ref.shape[1]
    near = len(out_refs)
    width = 2 * own_ref.shape[1]
    row = lax.broadcasted_iota(jnp.int32, (tokens, tokens), 0)
    column = lax.broadcasted_iota(jnp.int32, (tokens, tokens), 1)
    before = jnp.where(row < column, 1.0, 0.0).astype(jnp.bfloat16)
    live = lax.broadcasted_iota(jnp.int32, (1, tokens), 1) < live_count
    names = lax.broadcasted_iota(jnp.int32, (128, tokens), 0)
    slots = lax.broadcasted_iota(jnp.int32, (near, capacity, tokens), 1)
    ids = lax.broadcasted_iota(jnp.int32, (near, tokens), 0)
    near_experts = 2 * jnp.bitwise_xor(ids, member) + plane
    values = (
        (own_ref[...], away_ref[...]),
        (cross_ref[...], cross_away_ref[...]),
    )
    for which, source in enumerate((routes_ref, partner_ref)):
        picked = names < 0
        counted = ids < 0
        for k in range(source.shape[0]):
            route = source[k : k + 1, :]
            picked = picked | (names == route)
            counted = counted | (near_experts == route)
        counted = counted & live
        place = dot(jnp.where(counted, 1.0, 0.0).astype(jnp.bfloat16), before)
        place = jnp.where(counted, place.astype(jnp.int32), -1)
        hot = jnp.where(place[:, None, :] == slots, 1.0, 0.0).astype(jnp.bfloat16)
        hot = hot.reshape(near * capacity, tokens)
        hot_ref[which] = hot
        own, away = values[which]
        write_blocks(dot(hot, own), columns_of(plane, width, True), out_refs, capacity, which)
        write_blocks(dot(hot, away), columns_of(plane, width, False), out_refs, capacity, which)
        picked = jnp.where(picked, 1.0, 0.0).astype(jnp.bfloat16)
        write_blocks(
            dot(hot, picked, 1, 1), slice(width, width + 128), out_refs, capacity, which
        )


def dispatch_cot(
    facts, routes_t, partner_t, own, crossed, away, cross_away, near, capacity, expert_count
):
    tokens, half = own.shape
    out = jax.ShapeDtypeStruct((2 * capacity, 2 * half + 128), jnp.bfloat16)
    hot = jax.ShapeDtypeStruct((2, near * capacity, tokens), jnp.bfloat16)
    results = pl.pallas_call(
        functools.partial(dispatch_cot_kernel, capacity, expert_count),
        in_specs=[SMEM] + [VMEM] * 6,
        out_specs=[VMEM] * (1 + near),
        out_shape=[hot] + [out] * near,
        compiler_params=params(FULL),
        cost_estimate=cost(8 * near * capacity * tokens * half, 4 << 20),
        name="dispatch_cot",
    )(facts, routes_t, partner_t, own, crossed, away, cross_away)
    return results[0], results[1:]


def dispatch_rows_kernel(capacity, facts_ref, hot_ref, rows_ref, cross_ref, away_ref, *out_refs):
    plane = facts_ref[0]
    width = rows_ref.shape[1]
    write_blocks(dot(hot_ref[0], rows_ref[...]), slice(0, width), out_refs, capacity, 0)
    own, away = columns_of(plane, width, True), columns_of(plane, width, False)
    write_blocks(dot(hot_ref[1], cross_ref[...]), own, out_refs, capacity, 1)
    write_blocks(dot(hot_ref[1], away_ref[...]), away, out_refs, capacity, 1)


def dispatch_rows(facts, hot, rows, crossed, away, near, capacity):
    tokens, width = rows.shape
    out = jax.ShapeDtypeStruct((2 * capacity, width), jnp.bfloat16)
    return pl.pallas_call(
        functools.partial(dispatch_rows_kernel, capacity),
        in_specs=[SMEM] + [VMEM] * 4,
        out_specs=[VMEM] * near,
        out_shape=[out] * near,
        compiler_params=params(FULL),
        cost_estimate=cost(4 * near * capacity * tokens * width, 4 << 20),
        name="dispatch_rows",
    )(facts, hot, rows, crossed, away)


def combine_kernel(near, capacity, facts_ref, hot_ref, *refs):
    blocks = refs[:near]
    outs = refs[near : near + 4]
    gathered, sems = refs[near + 4 :]
    plane = facts_ref[0]
    width = gathered.shape[2]

    def copies(which):
        return [
            pltpu.make_async_copy(
                block.at[pl.ds(which * capacity, capacity)],
                gathered.at[which, pl.ds(j * capacity, capacity)],
                sems.at[which, j],
            )
            for j, block in enumerate(blocks)
        ]

    pending = [copies(0), copies(1)]
    for which in (1, 0):
        for copy in pending[which]:
            copy.start()
    for which in (1, 0):
        for copy in pending[which]:
            copy.wait()
        own_ref, away_ref = outs[2 * which : 2 * which + 2]
        for own, out_ref in ((True, own_ref), (False, away_ref)):
            columns = columns_of(plane, width, own)
            out_ref[...] = dot(hot_ref[which], gathered[which, :, columns], 0, 0).astype(
                out_ref.dtype
            )


def combine_rows(facts, hot, blocks, capacity):
    near = len(blocks)
    tokens, width = hot.shape[2], blocks[0].shape[1]
    own = jax.ShapeDtypeStruct((tokens, width // 2), jnp.float32)
    away = jax.ShapeDtypeStruct((tokens, width // 2), jnp.bfloat16)
    return pl.pallas_call(
        functools.partial(combine_kernel, near, capacity),
        in_specs=[SMEM, VMEM] + [ANY] * near,
        out_specs=[VMEM] * 4,
        out_shape=[own, away, own, away],
        scratch_shapes=[
            pltpu.VMEM((2, near * capacity, width), jnp.bfloat16),
            pltpu.SemaphoreType.DMA((2, near)),
        ],
        compiler_params=params(FULL),
        cost_estimate=cost(4 * near * capacity * tokens * width, 4 << 20),
        name="combine_rows",
    )(facts, hot, *blocks)


def expert_kernel(near, facts_ref, weights_ref, router_ref, *refs):
    row_blocks, cot_blocks = refs[:near], refs[near : 2 * near]
    refs = refs[2 * near :]
    back_blocks, moe_blocks = refs[:near], refs[near : 2 * near]
    rows_ref, hidden_ref, gate_grad_ref, up_grad_ref, slot_grad_ref, logits_ref = refs[
        2 * near : 2 * near + 6
    ]
    cot_all, back_all, moe_all, in_sems, out_sems = refs[2 * near + 6 :]
    index = pl.program_id(0)
    steps = pl.num_programs(0)
    block = row_blocks[0].shape[0]
    step = hidden_ref.shape[0]
    per_step = step // block

    def loads(j):
        place = pl.ds(j * block, block)
        return (
            pltpu.make_async_copy(row_blocks[j], rows_ref.at[place], in_sems.at[0, j]),
            pltpu.make_async_copy(cot_blocks[j], cot_all.at[place], in_sems.at[1, j]),
        )

    def stores(j):
        place = pl.ds(j * block, block)
        return (
            pltpu.make_async_copy(back_all.at[place], back_blocks[j], out_sems.at[0, j]),
            pltpu.make_async_copy(moe_all.at[place], moe_blocks[j], out_sems.at[1, j]),
        )

    @pl.when(index == 0)
    def _():
        for j in range(near):
            for copy in loads(j):
                copy.start()

    for s in range(near // per_step):

        @pl.when(index == s)
        def _():
            for j in range(s * per_step, (s + 1) * per_step):
                for copy in loads(j):
                    copy.wait()

    here = pl.ds(pl.multiple_of(index * step, step), step)
    width = rows_ref.shape[1]
    expert_count = router_ref.shape[0]
    rows = rows_ref[here, :]
    cot = cot_all[here, :width].astype(jnp.float32)
    picked = cot_all[here, width : width + 128][:, :expert_count]
    router = router_ref[...]
    logits = jnp.where(picked.astype(jnp.float32) > 0.5, dot(rows, router, 1, 1), NEGATIVE)
    terms = jnp.exp(logits - jnp.max(logits, axis=1, keepdims=True))
    gates = terms / jnp.sum(terms, axis=1, keepdims=True)
    expert = 2 * facts_ref[1] + facts_ref[0]
    own = (lax.broadcasted_iota(jnp.int32, gates.shape, 1) == expert).astype(jnp.float32)
    gate = jnp.sum(gates * own, axis=1, keepdims=True)

    def weight(f, i):
        value = weights_ref[:, f, i]
        return value.reshape(width, value.shape[-1])

    halves = range(weights_ref.shape[1])
    columns = weights_ref.shape[-1]
    kept = []
    out = 0.0
    for f in halves:
        gate_pre = dot(rows, weight(f, 0))
        up_pre = dot(rows, weight(f, 1))
        sigma = 1.0 / (1.0 + jnp.exp(-gate_pre))
        hidden = (gate_pre * sigma * up_pre).astype(jnp.bfloat16)
        hidden_ref[:, f * columns : (f + 1) * columns] = hidden
        out = out + dot(hidden, weight(f, 2), 1, 1)
        kept.append((gate_pre, up_pre, sigma))
    gate_grad = jnp.sum(out * cot, axis=1, keepdims=True)
    moe_all[here, :] = (gate * out).astype(jnp.bfloat16)
    slot_grad = (gate * cot).astype(jnp.bfloat16)
    slot_grad_ref[...] = slot_grad
    logits_grad = gate_grad * gate * (own - gates)
    upper = logits_grad.astype(jnp.bfloat16)
    lower = (logits_grad - upper.astype(jnp.float32)).astype(jnp.bfloat16)
    logits_ref[0] = upper
    logits_ref[1] = lower
    back = dot(upper, router) + dot(lower, router)
    for f in halves:
        gate_pre, up_pre, sigma = kept[f]
        hidden_grad = dot(slot_grad, weight(f, 2))
        gate_pre_grad = hidden_grad * up_pre * sigma * (1.0 + gate_pre * (1.0 - sigma))
        gate_pre_grad = gate_pre_grad.astype(jnp.bfloat16)
        up_pre_grad = (hidden_grad * gate_pre * sigma).astype(jnp.bfloat16)
        gate_grad_ref[:, f * columns : (f + 1) * columns] = gate_pre_grad
        up_grad_ref[:, f * columns : (f + 1) * columns] = up_pre_grad
        back = back + dot(gate_pre_grad, weight(f, 0), 1, 1)
        back = back + dot(up_pre_grad, weight(f, 1), 1, 1)
    back_all[here, :] = back.astype(jnp.bfloat16)

    for s in range(near // per_step):

        @pl.when(index == s)
        def _():
            for j in range(s * per_step, (s + 1) * per_step):
                for copy in stores(j):
                    copy.start()

    @pl.when(index == steps - 1)
    def _():
        for j in range(near):
            for copy in stores(j):
                copy.wait()


def run_expert(facts, row_blocks, cot_blocks, weights, router_t):
    near = len(row_blocks)
    block, width = row_blocks[0].shape
    count = near * block
    cot_width = cot_blocks[0].shape[1]
    hidden = 2 * weights.shape[-1]
    steps = 2
    step = count // steps
    bf16 = jnp.bfloat16
    row_block = lambda columns: pl.BlockSpec((step, columns), lambda i: (i, 0))
    whole = lambda value: pl.BlockSpec(value.shape, lambda i: (0,) * value.ndim)
    experts = router_t.shape[0]
    block_shape = jax.ShapeDtypeStruct((block, width), bf16)
    results = pl.pallas_call(
        functools.partial(expert_kernel, near),
        grid=(steps,),
        in_specs=[SMEM, whole(weights), whole(router_t)] + [ANY] * (2 * near),
        out_specs=[ANY] * (2 * near)
        + [
            pl.BlockSpec((count, width), lambda i: (0, 0)),
            row_block(hidden),
            row_block(hidden),
            row_block(hidden),
            row_block(width),
            pl.BlockSpec((2, step, experts), lambda i: (0, i, 0)),
        ],
        out_shape=[block_shape] * (2 * near)
        + [
            jax.ShapeDtypeStruct((count, width), bf16),
            jax.ShapeDtypeStruct((count, hidden), bf16),
            jax.ShapeDtypeStruct((count, hidden), bf16),
            jax.ShapeDtypeStruct((count, hidden), bf16),
            jax.ShapeDtypeStruct((count, width), bf16),
            jax.ShapeDtypeStruct((2, count, experts), bf16),
        ],
        scratch_shapes=[
            pltpu.VMEM((count, cot_width), bf16),
            pltpu.VMEM((count, width), bf16),
            pltpu.VMEM((count, width), bf16),
            pltpu.SemaphoreType.DMA((2, near)),
            pltpu.SemaphoreType.DMA((2, near)),
        ],
        compiler_params=params(FULL),
        cost_estimate=cost(12 * count * width * hidden, 16 << 20, count * hidden),
        name="expert_rows",
    )(facts, weights, router_t, *row_blocks, *cot_blocks)
    return results[:near], results[near : 2 * near], results[2 * near :]


def put_grad(piece, out_ref, place=()):
    blocks, planes, block_rows, columns = (
        out_ref.shape[0],
        out_ref.shape[1],
        out_ref.shape[-2],
        out_ref.shape[-1],
    )
    piece = piece.astype(jnp.bfloat16)
    for f in range(planes):
        out_ref[(slice(None), f) + place] = piece[:, f * columns : (f + 1) * columns].reshape(
            blocks, block_rows, columns
        )


def grads_kernel(
    rows_ref,
    hidden_ref,
    gate_grad_ref,
    up_grad_ref,
    slot_grad_ref,
    logits_ref,
    pair_ref,
    down_ref,
    router_ref,
):
    rows = rows_ref[...]
    put_grad(dot(slot_grad_ref[...], hidden_ref[...], 0, 0), down_ref)
    put_grad(dot(rows, gate_grad_ref[...], 0, 0), pair_ref, (0,))
    put_grad(dot(rows, up_grad_ref[...], 0, 0), pair_ref, (1,))
    router_ref[...] = dot(logits_ref[0], rows, 0, 0) + dot(logits_ref[1], rows, 0, 0)


def run_grads(rows, hidden, gate_grad, up_grad, slot_grad, logits, shape):
    count, width = rows.shape
    steps = 4
    step = width // steps
    experts = logits.shape[2]
    blocks, planes, tail = shape[0] // steps, shape[1], shape[2:]
    column = pl.BlockSpec((count, step), lambda i: (0, i))
    whole = lambda value: pl.BlockSpec(value.shape, lambda i: (0,) * value.ndim)
    return pl.pallas_call(
        grads_kernel,
        grid=(steps,),
        in_specs=[column, whole(hidden), whole(gate_grad), whole(up_grad), column, whole(logits)],
        out_specs=[
            pl.BlockSpec((blocks, planes, 2) + tail, lambda i: (i, 0, 0, 0, 0)),
            pl.BlockSpec((blocks, planes) + tail, lambda i: (i, 0, 0, 0)),
            pl.BlockSpec((experts, step), lambda i: (0, i)),
        ],
        out_shape=[
            jax.ShapeDtypeStruct(shape[:2] + (2,) + tail, jnp.bfloat16),
            jax.ShapeDtypeStruct(shape, jnp.bfloat16),
            jax.ShapeDtypeStruct((experts, width), jnp.float32),
        ],
        compiler_params=params(FULL),
        cost_estimate=cost(6 * count * math.prod(shape), 12 << 20),
        name="expert_grads",
    )(rows, hidden, gate_grad, up_grad, slot_grad, logits)


def tables_kernel(place_ref, placement_ref, lengths_ref, facts_ref, cos_ref, sin_ref):
    holder = lax.fori_loop(
        0,
        placement_ref.shape[0],
        lambda i, total: total + jnp.where(placement_ref[i] == place_ref[1], i, 0),
        jnp.int32(0),
    )
    facts_ref[0] = place_ref[0]
    facts_ref[1] = place_ref[2]
    rows, lanes = cos_ref.shape
    row = lax.broadcasted_iota(jnp.int32, (rows, lanes), 0)
    start = jnp.zeros((rows, lanes), jnp.int32)
    end = jnp.int32(0)
    count = lengths_ref.shape[0]
    for j in range(count):
        end = end + lengths_ref[j, holder]
        facts_ref[3 + j] = end
        start = jnp.where(row >= end, end, start)
    facts_ref[2] = end
    half = HEAD_DIM // 2
    lane = lax.broadcasted_iota(jnp.int32, (rows, lanes), 1)
    index = jnp.bitwise_and(lane, half - 1).astype(jnp.float32)
    frequency = jnp.exp(-(2.0 * index / (2.0 * half)) * math.log(ROPE_BASE))
    angles = (row - start).astype(jnp.float32) * frequency
    cos_ref[...] = jnp.cos(angles)
    sine = jnp.sin(angles)
    sin_ref[...] = jnp.where(jnp.bitwise_and(lane, half) == 0, -sine, sine)


def make_tables(place, placement, lengths_t, rows):
    table = jax.ShapeDtypeStruct((rows, 128), jnp.float32)
    return pl.pallas_call(
        tables_kernel,
        in_specs=[SMEM, SMEM, SMEM],
        out_specs=[SMEM, VMEM, VMEM],
        out_shape=[
            jax.ShapeDtypeStruct((3 + lengths_t.shape[0],), jnp.int32),
            table,
            table,
        ],
        compiler_params=params(FULL),
        cost_estimate=cost(1 << 20, 1 << 18, rows * 256),
        name="tables",
    )(place, placement, lengths_t)


def turn(values, cos, sine):
    half = HEAD_DIM // 2
    lane = lax.broadcasted_iota(jnp.int32, cos.shape, 1)
    first = jnp.bitwise_and(lane, half) == 0
    pieces = []
    for c in range(values.shape[1] // 128):
        piece = values[:, c * 128 : (c + 1) * 128]
        other = jnp.where(first, pltpu.roll(piece, 128 - half, 1), pltpu.roll(piece, half, 1))
        pieces.append(piece * cos + other * sine)
    return jnp.concatenate(pieces, axis=1)


def allowed_pairs(facts_ref, rows):
    query = lax.broadcasted_iota(jnp.int32, (rows, rows), 0)
    key = lax.broadcasted_iota(jnp.int32, (rows, rows), 1)
    start = jnp.zeros((rows, rows), jnp.int32)
    for j in range(3, facts_ref.shape[0]):
        start = jnp.where(query >= facts_ref[j], facts_ref[j], start)
    return (key <= query) & (key >= start)


def pair_heads(values, g):
    chunk = values[:, 2 * g * HEAD_DIM : 2 * (g + 1) * HEAD_DIM]
    return jnp.concatenate([chunk[:, :HEAD_DIM], chunk[:, HEAD_DIM:]], axis=0)


def unpair_heads(values):
    rows = values.shape[0] // 2
    return jnp.concatenate([values[:rows], values[rows:]], axis=1)


def pair_scores(query, key, allowed):
    scores = dot(query, key, 1, 1) * (1.0 / HEAD_DIM)
    return jnp.where(jnp.concatenate([allowed, allowed], axis=0), scores, NEGATIVE)


def put_halves(ref, plane, own, away):
    width = ref.shape[1]
    ref[:, columns_of(plane, width, True)] = own
    ref[:, columns_of(plane, width, False)] = away


def inverse_norm(values):
    mean = jnp.mean(values * values, axis=1, keepdims=True)
    return lax.rsqrt(mean + EPSILON)


def attend_kernel(
    facts_ref,
    own_ref,
    away_ref,
    gain_ref,
    query_w_ref,
    key_w_ref,
    value_w_ref,
    output_w_ref,
    cos_ref,
    sin_ref,
    part_ref,
    normed_ref,
    query_ref,
    key_ref,
    value_ref,
    context_ref,
    total_ref,
    wide,
):
    put_halves(
        wide, facts_ref[0], own_ref[...].astype(jnp.float32), away_ref[...].astype(jnp.float32)
    )
    values = wide[...]
    rows = values.shape[0]
    normed = (values * inverse_norm(values) * gain_ref[...]).astype(jnp.bfloat16)
    normed_ref[...] = normed
    cos, sine = cos_ref[...], sin_ref[...]
    query = turn(dot(normed, query_w_ref[...]), cos, sine).astype(jnp.bfloat16)
    key = turn(dot(normed, key_w_ref[...]), cos, sine).astype(jnp.bfloat16)
    value = dot(normed, value_w_ref[...]).astype(jnp.bfloat16)
    query_ref[...] = query
    key_ref[...] = key
    value_ref[...] = value
    allowed = allowed_pairs(facts_ref, rows)
    live = lax.broadcasted_iota(jnp.int32, (rows, 2 * HEAD_DIM), 0) < facts_ref[2]
    pieces, totals = [], []
    for g in range(key.shape[1] // HEAD_DIM):
        place = slice(g * HEAD_DIM, (g + 1) * HEAD_DIM)
        scores = pair_scores(pair_heads(query, g), key[:, place], allowed)
        top = jnp.max(scores, axis=1, keepdims=True)
        terms = jnp.exp(scores - top)
        total = jnp.sum(terms, axis=1, keepdims=True)
        probs = (terms / total).astype(jnp.bfloat16)
        context = unpair_heads(dot(probs, value[:, place]))
        pieces.append(jnp.where(live, context, 0.0).astype(jnp.bfloat16))
        log_total = top + jnp.log(total)
        totals += [log_total[:rows], log_total[rows:]]
    context = jnp.concatenate(pieces, axis=1)
    context_ref[...] = context
    lane = lax.broadcasted_iota(jnp.int32, (rows, 128), 1)
    packed = jnp.zeros((rows, 128), jnp.float32)
    for h, log_total in enumerate(totals):
        packed = jnp.where(lane == h, log_total, packed)
    total_ref[...] = packed
    part_ref[...] = dot(context, output_w_ref[...]).astype(jnp.bfloat16)


def attend(facts, own, away, gain, query_w, key_w, value_w, output_w, cos, sine):
    rows = own.shape[0]
    width = 2 * own.shape[1]
    low = lambda columns: jax.ShapeDtypeStruct((rows, columns), jnp.bfloat16)
    return pl.pallas_call(
        attend_kernel,
        in_specs=[SMEM] + [VMEM] * 9,
        out_specs=[VMEM] * 7,
        out_shape=[
            low(width),
            low(width),
            low(query_w.shape[1]),
            low(key_w.shape[1]),
            low(value_w.shape[1]),
            low(query_w.shape[1]),
            jax.ShapeDtypeStruct((rows, 128), jnp.float32),
        ],
        scratch_shapes=[pltpu.VMEM((rows, width), jnp.float32)],
        compiler_params=params(FULL),
        cost_estimate=cost(8 * rows * width * width // 2, 8 << 20, rows * rows * 8),
        name="attend",
    )(facts, own, away, gain, query_w, key_w, value_w, output_w, cos, sine)


def mix_kernel(
    facts_ref, own_ref, away_ref, part_ref, recv_ref, gain_ref, residual_ref, mixed_ref, half_ref
):
    plane = facts_ref[0]
    put_halves(
        residual_ref, plane, own_ref[...].astype(jnp.float32), away_ref[...].astype(jnp.float32)
    )
    residual = residual_ref[...] + (
        part_ref[...].astype(jnp.float32) + recv_ref[...].astype(jnp.float32)
    )
    residual_ref[...] = residual
    mixed_ref[...] = (residual * inverse_norm(residual) * gain_ref[...]).astype(jnp.bfloat16)
    half_ref[...] = mixed_ref[:, columns_of(plane, residual.shape[1], True)]


def mix(facts, own, away, part, recv, gain):
    rows, width = part.shape
    return pl.pallas_call(
        mix_kernel,
        in_specs=[SMEM] + [VMEM] * 5,
        out_specs=[VMEM] * 3,
        out_shape=[
            jax.ShapeDtypeStruct((rows, width), jnp.float32),
            jax.ShapeDtypeStruct((rows, width), jnp.bfloat16),
            jax.ShapeDtypeStruct((rows, width // 2), jnp.bfloat16),
        ],
        compiler_params=params(FULL),
        cost_estimate=cost(rows * width * 8, 3 << 20),
        name="mix",
    )(facts, own, away, part, recv, gain)


def attend_back_kernel(
    facts_ref,
    mixed_ref,
    mixed_away_ref,
    cot_ref,
    cot_away_ref,
    residual_ref,
    own_ref,
    away_ref,
    gain_ref,
    expert_gain_ref,
    normed_ref,
    query_ref,
    key_ref,
    value_ref,
    context_ref,
    total_ref,
    query_w_ref,
    key_w_ref,
    value_w_ref,
    output_w_ref,
    cos_ref,
    sin_ref,
    router_ref,
    parts_ref,
    normed_own_ref,
    normed_away_ref,
    base_ref,
    inner_ref,
    wide,
):
    plane = facts_ref[0]
    own_columns = columns_of(plane, wide.shape[1], True)
    away_columns = columns_of(plane, wide.shape[1], False)
    rows, width = wide.shape

    put_halves(
        wide, plane, mixed_ref[...].astype(jnp.float32), mixed_away_ref[...].astype(jnp.float32)
    )
    mixed_grad = wide[...]
    put_halves(
        wide, plane, cot_ref[...].astype(jnp.float32), cot_away_ref[...].astype(jnp.float32)
    )
    residual = residual_ref[...]
    inverse = inverse_norm(residual)
    scaled = mixed_grad * expert_gain_ref[...]
    mean = jnp.mean(scaled * residual, axis=1, keepdims=True)
    residual_grad = (
        wide[...] + inverse * scaled - residual * (inverse * inverse * inverse * mean)
    )
    expert_gain_grad = 0.5 * jnp.sum(mixed_grad * residual * inverse, axis=0, keepdims=True)
    wide[...] = residual_grad
    base_ref[...] = wide[:, own_columns]
    low = residual_grad.astype(jnp.bfloat16)
    context = context_ref[...]
    columns = context.shape[1]
    parts_ref[:, :columns] = dot(low, context, 0, 0).astype(parts_ref.dtype)
    live = lax.broadcasted_iota(jnp.int32, (rows, columns), 0) < facts_ref[2]
    context_grad = jnp.where(live, dot(low, output_w_ref[...], 1, 1), 0.0).astype(jnp.bfloat16)

    query, key, value = query_ref[...], key_ref[...], value_ref[...]
    totals = total_ref[...]
    allowed = allowed_pairs(facts_ref, rows)
    scale = 1.0 / HEAD_DIM
    query_grads, key_grads, value_grads = [], [], []
    for g in range(key.shape[1] // HEAD_DIM):
        place = slice(g * HEAD_DIM, (g + 1) * HEAD_DIM)
        pair = pair_heads(query, g)
        pair_grad = pair_heads(context_grad, g)
        total = jnp.concatenate([totals[:, 2 * g : 2 * g + 1], totals[:, 2 * g + 1 : 2 * g + 2]])
        probs = jnp.exp(pair_scores(pair, key[:, place], allowed) - total)
        prob_grad = dot(pair_grad, value[:, place], 1, 1)
        inner = jnp.sum(probs * prob_grad, axis=1, keepdims=True)
        score_grad = (probs * (prob_grad - inner)).astype(jnp.bfloat16)
        query_grads.append(unpair_heads(dot(score_grad, key[:, place]) * scale))
        key_grads.append(dot(score_grad, pair, 0, 0) * scale)
        value_grads.append(dot(probs.astype(jnp.bfloat16), pair_grad, 0, 0))
    cos, sine = cos_ref[...], -sin_ref[...]
    query_grad = turn(jnp.concatenate(query_grads, axis=1), cos, sine).astype(jnp.bfloat16)
    key_grad = turn(jnp.concatenate(key_grads, axis=1), cos, sine).astype(jnp.bfloat16)
    value_grad = jnp.concatenate(value_grads, axis=1).astype(jnp.bfloat16)
    normed_t = normed_ref[...]
    start = columns
    for grad in (query_grad, key_grad, value_grad):
        size = grad.shape[1]
        parts_ref[:, start : start + size] = dot(normed_t, grad, 0, 0).astype(parts_ref.dtype)
        start += size
    normed_grad = (
        dot(query_grad, query_w_ref[...], 1, 1)
        + dot(key_grad, key_w_ref[...], 1, 1)
        + dot(value_grad, value_w_ref[...], 1, 1)
    )
    put_halves(
        wide, plane, own_ref[...].astype(jnp.float32), away_ref[...].astype(jnp.float32)
    )
    values = wide[...]
    product = normed_grad * values
    gain_grad = jnp.sum(product * inverse_norm(values), axis=0, keepdims=True)
    inner = jnp.sum(product * gain_ref[...], axis=1, keepdims=True)
    inner_ref[...] = jnp.broadcast_to(inner, (rows, 128)).T[: inner_ref.shape[0]]
    wide[...] = normed_grad
    normed_own_ref[...] = wide[:, own_columns]
    normed_away_ref[...] = wide[:, away_columns].astype(jnp.bfloat16)
    experts = router_ref.shape[0]
    rest = jnp.zeros((128 - experts - 2, width), jnp.float32)
    packed = jnp.concatenate([router_ref[...], gain_grad, expert_gain_grad, rest], axis=0)
    parts_ref[:, start : start + 128] = packed.T.astype(parts_ref.dtype)


def attend_back(facts, *values):
    mixed, query_w, key_w, value_w = values[0], values[15], values[16], values[17]
    rows, half = mixed.shape
    width = 2 * half
    columns = 2 * query_w.shape[1] + key_w.shape[1] + value_w.shape[1] + 128
    wide = lambda columns, kind: jax.ShapeDtypeStruct((rows, columns), kind)
    return pl.pallas_call(
        attend_back_kernel,
        in_specs=[SMEM] + [VMEM] * len(values),
        out_specs=[VMEM] * 5,
        out_shape=[
            jax.ShapeDtypeStruct((width, columns), jnp.bfloat16),
            wide(half, jnp.float32),
            wide(half, jnp.bfloat16),
            wide(half, jnp.float32),
            jax.ShapeDtypeStruct((8, rows), jnp.float32),
        ],
        scratch_shapes=[pltpu.VMEM((rows, width), jnp.float32)],
        compiler_params=params(FULL),
        cost_estimate=cost(16 * rows * width * half * 2, 14 << 20, rows * rows * 8),
        name="attend_back",
    )(facts, *values)


def finish_kernel(
    facts_ref,
    own_ref,
    away_ref,
    gain_ref,
    residual_ref,
    moe_ref,
    moe_recv_ref,
    moe_cross_ref,
    base_ref,
    normed_ref,
    normed_recv_ref,
    inner_ref,
    inner_recv_ref,
    out_ref,
):
    rows, half = own_ref.shape
    own_columns = columns_of(facts_ref[0], 2 * half, True)
    own = own_ref[...].astype(jnp.float32)
    away = away_ref[...].astype(jnp.float32)
    total = jnp.sum(own * own, axis=1, keepdims=True) + jnp.sum(away * away, axis=1, keepdims=True)
    inverse = lax.rsqrt(total / (2 * half) + EPSILON)
    inner = (inner_ref[0:1, :] + inner_recv_ref[0:1, :]) / (2 * half)
    inner = jnp.broadcast_to(inner, (128, rows)).T[:, :1]
    normed = normed_ref[...] + normed_recv_ref[...].astype(jnp.float32)
    grad = (
        base_ref[...]
        + inverse * normed * gain_ref[:, own_columns]
        - own * (inverse * inverse * inverse * inner)
    )
    moe = (
        moe_ref[...]
        + moe_recv_ref[...].astype(jnp.float32)
        + moe_cross_ref[...].astype(jnp.float32)
    )
    out_ref[:, :half] = (residual_ref[:, own_columns] + moe).astype(out_ref.dtype)
    out_ref[:, half:] = grad.astype(out_ref.dtype)


def finish(facts, *values):
    rows, half = values[0].shape
    return pl.pallas_call(
        finish_kernel,
        in_specs=[SMEM] + [VMEM] * len(values),
        out_specs=VMEM,
        out_shape=jax.ShapeDtypeStruct((rows, 2 * half), jnp.bfloat16),
        compiler_params=params(FULL),
        cost_estimate=cost(rows * half * 16, 4 << 20),
        name="finish",
    )(facts, *values)


def local(
    inputs,
    cotangent,
    attn_gain,
    expert_gain,
    query_weight,
    key_weight,
    value_weight,
    output_weight,
    router_weight,
    gate_weight,
    up_weight,
    down_weight,
    routes,
    lengths,
    placement,
):
    row_count, top_count = routes.shape
    expert_count = router_weight.shape[1]
    capacity = row_count * top_count // expert_count
    kv_local = key_weight.shape[1] // HEAD_DIM
    heads_local = query_weight.shape[1] // HEAD_DIM
    group = heads_local // kv_local
    scale = 1.0 / HEAD_DIM
    width_half = inputs.shape[1]
    width = 2 * width_half
    plane = lax.axis_index("tensor")
    devices = lax.axis_size("dp")
    dp_index = lax.axis_index("dp")
    members = expert_count // 2
    near = members // 2
    clusters = devices // members
    member = dp_index % members
    expert = 2 * member + plane
    inside = [[c * members + m for m in range(members)] for c in range(clusters)]
    across = [[c * members + m for c in range(clusters)] for m in range(members)]

    def cross(values):
        return lax.ppermute(values, "dp", [(i, i ^ near) for i in range(devices)])

    def spread(blocks):
        return [blocks[0]] + [
            lax.ppermute(blocks[s], "dp", [(i, i ^ s) for i in range(devices)])
            for s in range(1, near)
        ]

    def halves(values, axis):
        size = values.shape[axis] // 2
        return (
            lax.dynamic_slice_in_dim(values, plane * size, size, axis),
            lax.dynamic_slice_in_dim(values, (1 - plane) * size, size, axis),
        )

    def join(own, other, axis):
        first = jnp.where(plane == 0, own, other)
        second = jnp.where(plane == 0, other, own)
        return jnp.concatenate([first, second], axis=axis)

    def add_planes(part):
        low = part.astype(jnp.bfloat16)
        return low.astype(jnp.float32) + swap_tensor(low).astype(jnp.float32)

    routes_t = routes.T
    away = swap_tensor(inputs)
    partner_t = cross(routes_t)
    cot_cross = cross(cotangent)
    cot_away = swap_tensor(cotangent)
    cot_cross_away = swap_tensor(cot_cross)
    place = jnp.stack([plane, dp_index, member]).astype(jnp.int32)
    facts, cos_table, sin_table = make_tables(place, placement, lengths.T, row_count)
    gain_one, gain_two = attn_gain[None], expert_gain[None]
    attn_part, normed, query, key, value, context, log_total = attend(
        facts,
        inputs,
        away,
        gain_one,
        query_weight,
        key_weight,
        value_weight,
        output_weight,
        cos_table,
        sin_table,
    )

    def to_owner(values):
        if clusters == 1:
            owned = lax.all_to_all(
                values, ("dp", "tensor"), split_axis=0, concat_axis=0, tiled=True
            )
            return owned.reshape((devices, 2) + owned.shape[1:])
        by_plane = values.reshape((members, 2) + values.shape[1:])
        own_w = lax.dynamic_index_in_dim(by_plane, plane, 1, keepdims=False)
        other_w = swap_tensor(lax.dynamic_index_in_dim(by_plane, 1 - plane, 1, keepdims=False))
        owned = jnp.stack(
            [jnp.where(plane == 0, own_w, other_w), jnp.where(plane == 0, other_w, own_w)], axis=1
        )
        owned = lax.all_to_all(
            owned, "dp", split_axis=0, concat_axis=0, tiled=True, axis_index_groups=inside
        )
        owned = lax.all_gather(owned, "dp", axis=0, tiled=True, axis_index_groups=across)
        owned = owned.reshape((members, clusters) + owned.shape[1:])
        owned = jnp.moveaxis(owned, 1, -3)
        return owned.reshape(owned.shape[:-3] + (-1, owned.shape[-1]))

    def from_owner(values):
        if clusters == 1:
            return lax.all_to_all(
                values.reshape((2 * devices,) + values.shape[2:]),
                ("dp", "tensor"),
                split_axis=0,
                concat_axis=0,
                tiled=True,
            )
        values = values.reshape(values.shape[:-2] + (clusters, -1, values.shape[-1]))
        values = jnp.moveaxis(values, -3, 1)
        values = values.reshape((devices,) + values.shape[2:])
        values = lax.psum_scatter(
            values, "dp", scatter_dimension=0, tiled=True, axis_index_groups=across
        )
        values = lax.all_to_all(
            values, "dp", split_axis=0, concat_axis=0, tiled=True, axis_index_groups=inside
        )
        own_g = lax.dynamic_index_in_dim(values, plane, 1, keepdims=False)
        other_g = swap_tensor(lax.dynamic_index_in_dim(values, 1 - plane, 1, keepdims=False))
        values = jnp.stack(
            [jnp.where(plane == 0, own_g, other_g), jnp.where(plane == 0, other_g, own_g)], axis=1
        )
        return values.reshape((expert_count,) + values.shape[2:])

    owned = to_owner(
        after(
            jnp.stack([gate_weight, up_weight, jnp.swapaxes(down_weight, 1, 2)], axis=1),
            away,
            partner_t,
            cot_away,
            cot_cross,
        )
    )

    hot, cot_blocks = dispatch_cot(
        facts,
        routes_t,
        partner_t,
        cotangent,
        cot_cross,
        cot_away,
        cot_cross_away,
        near,
        capacity,
        expert_count,
    )
    cot_blocks = spread(cot_blocks)

    def combine(hot, blocks):
        mine, mine_away, others, others_away = combine_rows(facts, hot, blocks, capacity)
        others = others + swap_tensor(others_away).astype(jnp.float32)
        return mine, swap_tensor(mine_away), cross(others.astype(jnp.bfloat16))

    residual, mixed_rows, mixed_half = mix(
        facts, inputs, away, attn_part, swap_tensor(attn_part), gain_two
    )
    mixed_cross = cross(mixed_half)
    mixed_away = swap_tensor(mixed_cross)
    row_blocks = spread(
        dispatch_rows(
            facts, after(hot, *cot_blocks[1:7]), mixed_rows, mixed_cross, mixed_away, near, capacity
        )
    )

    back_blocks, moe_blocks, kept = run_expert(
        facts, row_blocks, cot_blocks, owned, router_weight.T
    )
    back_blocks = spread(back_blocks)
    pair_part, down_part, router_part = run_grads(
        *kept, (members, 2, width // members, gate_weight.shape[2])
    )
    down_share = from_owner(down_part)
    moe_blocks = spread(moe_blocks)
    mine, mine_recv, mine_cross = combine(after(hot, down_share), back_blocks)
    mixed_half = mine + mine_recv.astype(jnp.float32) + mine_cross.astype(jnp.float32)
    mixed_half = mixed_half.astype(jnp.bfloat16)
    mixed_away = swap_tensor(mixed_half)
    pair_share = from_owner(after(pair_part, mixed_half))
    moe_parts = combine(hot, moe_blocks)

    parts, normed_own, normed_away, base_half, inner = attend_back(
        facts,
        mixed_half,
        mixed_away,
        cotangent,
        cot_away,
        after(residual, *moe_blocks),
        inputs,
        away,
        gain_one,
        gain_two,
        normed,
        query,
        key,
        value,
        context,
        log_total,
        query_weight,
        key_weight,
        value_weight,
        output_weight,
        cos_table,
        sin_table,
        router_part,
    )
    share = lax.psum_scatter(parts, "dp", scatter_dimension=0, tiled=True)
    cuts = [context.shape[1]]
    for w in (query_weight, key_weight, value_weight):
        cuts.append(cuts[-1] + w.shape[1])
    small = share[:, cuts[3] :]
    small = small.astype(jnp.float32) + swap_tensor(small).astype(jnp.float32)
    share = share.astype(jnp.float32)
    output_part = share[:, : cuts[0]].T
    query_part = share[:, cuts[0] : cuts[1]]
    key_part = share[:, cuts[1] : cuts[2]]
    value_part = share[:, cuts[2] : cuts[3]]
    router_share = small[:, :expert_count]
    attn_gain_part = small[:, expert_count]
    expert_gain_part = small[:, expert_count + 1]

    gate_w_part = pair_share[:, 0].astype(jnp.float32)
    up_w_part = pair_share[:, 1].astype(jnp.float32)
    down_w_part = jnp.swapaxes(down_share, 1, 2).astype(jnp.float32)

    piece_rows = row_count // devices
    moved = finish(
        facts,
        inputs,
        away,
        gain_one,
        residual,
        *moe_parts,
        base_half,
        normed_own,
        swap_tensor(normed_away),
        inner,
        swap_tensor(inner),
    )
    moved = after(moved, pair_share)
    moved = lax.all_to_all(
        moved.reshape(devices, piece_rows, width), "dp", split_axis=0, concat_axis=0, tiled=True
    )
    moved = jnp.take(moved, placement, axis=0)
    moved = lax.all_to_all(moved, "dp", split_axis=0, concat_axis=0, tiled=True)
    moved = moved.reshape(row_count, width)
    outputs = moved[:, :width_half]
    input_result = moved[:, width_half:].astype(jnp.float32)
    return (
        outputs,
        input_result,
        attn_gain_part,
        expert_gain_part,
        query_part,
        key_part,
        value_part,
        output_part,
        router_share,
        gate_w_part,
        up_w_part,
        down_w_part,
    )


def solution(mesh):
    in_specs = (
        P("dp", "tensor"),
        P("dp", "tensor"),
        P(),
        P(),
        P(None, "tensor"),
        P(None, "tensor"),
        P(None, "tensor"),
        P("tensor", None),
        P(),
        P(None, "dp", "tensor"),
        P(None, "dp", "tensor"),
        P(None, "tensor", "dp"),
        P("dp", None),
        P(),
        P(),
    )
    out_specs = (
        P("dp", "tensor"),
        P("dp", "tensor"),
        P("dp"),
        P("dp"),
        P("dp", "tensor"),
        P("dp", "tensor"),
        P("dp", "tensor"),
        P("tensor", "dp"),
        P("dp", None),
        P(None, "dp", "tensor"),
        P(None, "dp", "tensor"),
        P(None, "tensor", "dp"),
    )
    return jax.shard_map(local, mesh=mesh, in_specs=in_specs, out_specs=out_specs, check_vma=False)
```

```python
import functools
import math

import jax
import jax.numpy as jnp
from jax import lax
from jax.experimental import pallas as pl
from jax.experimental.pallas import tpu as pltpu
from jax.sharding import PartitionSpec as P

HEAD_DIM = 64


EPSILON = 1e-06
ROPE_BASE = 10000.0
NEGATIVE = -1e30


def swap_tensor(values):
    return lax.ppermute(values, "tensor", [(0, 1), (1, 0)])


def mm(left, right, contract):
    return lax.dot_general(
        left, right, ((contract[:1], contract[1:]), ((), ())), preferred_element_type=jnp.float32
    )


def after(values, *others):
    return lax.optimization_barrier((values,) + others)[0]


def dot(left, right, left_axis=1, right_axis=0):
    return lax.dot_general(
        left,
        right,
        (((left_axis,), (right_axis,)), ((), ())),
        preferred_element_type=jnp.float32,
    )


def params(megabytes):
    return pltpu.CompilerParams(vmem_limit_bytes=megabytes << 20)


def cost(flops, size, transcendentals=0):
    return pl.CostEstimate(
        flops=flops, bytes_accessed=size, transcendentals=transcendentals
    )


SMEM = pl.BlockSpec(memory_space=pltpu.SMEM)
VMEM = pl.BlockSpec(memory_space=pltpu.VMEM)
ANY = pl.BlockSpec(memory_space=pl.ANY)
FULL = 60


def columns_of(plane, width, own):
    half = width // 2
    start = plane * half if own else (1 - plane) * half
    return pl.ds(pl.multiple_of(start, half), half)


def write_blocks(product, columns, out_refs, capacity, which):
    for j, out_ref in enumerate(out_refs):
        out_ref[which * capacity : (which + 1) * capacity, columns] = product[
            j * capacity : (j + 1) * capacity
        ].astype(out_ref.dtype)


def dispatch_cot_kernel(capacity, expert_count, facts_ref, routes_ref, partner_ref, *refs):
    own_ref, cross_ref, away_ref, cross_away_ref, hot_ref = refs[:5]
    out_refs = refs[5:]
    plane, member, live_count = facts_ref[0], facts_ref[1], facts_ref[2]
    tokens = routes_ref.shape[1]
    near = len(out_refs)
    width = 2 * own_ref.shape[1]
    row = lax.broadcasted_iota(jnp.int32, (tokens, tokens), 0)
    column = lax.broadcasted_iota(jnp.int32, (tokens, tokens), 1)
    before = jnp.where(row < column, 1.0, 0.0).astype(jnp.bfloat16)
    live = lax.broadcasted_iota(jnp.int32, (1, tokens), 1) < live_count
    names = lax.broadcasted_iota(jnp.int32, (128, tokens), 0)
    slots = lax.broadcasted_iota(jnp.int32, (near, capacity, tokens), 1)
    ids = lax.broadcasted_iota(jnp.int32, (near, tokens), 0)
    near_experts = 2 * jnp.bitwise_xor(ids, member) + plane
    values = (
        (own_ref[...], away_ref[...]),
        (cross_ref[...], cross_away_ref[...]),
    )
    for which, source in enumerate((routes_ref, partner_ref)):
        picked = names < 0
        counted = ids < 0
        for k in range(source.shape[0]):
            route = source[k : k + 1, :]
            picked = picked | (names == route)
            counted = counted | (near_experts == route)
        counted = counted & live
        place = dot(jnp.where(counted, 1.0, 0.0).astype(jnp.bfloat16), before)
        place = jnp.where(counted, place.astype(jnp.int32), -1)
        hot = jnp.where(place[:, None, :] == slots, 1.0, 0.0).astype(jnp.bfloat16)
        hot = hot.reshape(near * capacity, tokens)
        hot_ref[which] = hot
        own, away = values[which]
        write_blocks(dot(hot, own), columns_of(plane, width, True), out_refs, capacity, which)
        write_blocks(dot(hot, away), columns_of(plane, width, False), out_refs, capacity, which)
        picked = jnp.where(picked, 1.0, 0.0).astype(jnp.bfloat16)
        write_blocks(
            dot(hot, picked, 1, 1), slice(width, width + 128), out_refs, capacity, which
        )


def dispatch_cot(
    facts, routes_t, partner_t, own, crossed, away, cross_away, near, capacity, expert_count
):
    tokens, half = own.shape
    out = jax.ShapeDtypeStruct((2 * capacity, 2 * half + 128), jnp.bfloat16)
    hot = jax.ShapeDtypeStruct((2, near * capacity, tokens), jnp.bfloat16)
    results = pl.pallas_call(
        functools.partial(dispatch_cot_kernel, capacity, expert_count),
        in_specs=[SMEM] + [VMEM] * 6,
        out_specs=[VMEM] * (1 + near),
        out_shape=[hot] + [out] * near,
        compiler_params=params(FULL),
        cost_estimate=cost(8 * near * capacity * tokens * half, 4 << 20),
        name="dispatch_cot",
    )(facts, routes_t, partner_t, own, crossed, away, cross_away)
    return results[0], results[1:]


def dispatch_rows_kernel(capacity, facts_ref, hot_ref, rows_ref, cross_ref, away_ref, *out_refs):
    plane = facts_ref[0]
    width = rows_ref.shape[1]
    write_blocks(dot(hot_ref[0], rows_ref[...]), slice(0, width), out_refs, capacity, 0)
    own, away = columns_of(plane, width, True), columns_of(plane, width, False)
    write_blocks(dot(hot_ref[1], cross_ref[...]), own, out_refs, capacity, 1)
    write_blocks(dot(hot_ref[1], away_ref[...]), away, out_refs, capacity, 1)


def dispatch_rows(facts, hot, rows, crossed, away, near, capacity):
    tokens, width = rows.shape
    out = jax.ShapeDtypeStruct((2 * capacity, width), jnp.bfloat16)
    return pl.pallas_call(
        functools.partial(dispatch_rows_kernel, capacity),
        in_specs=[SMEM] + [VMEM] * 4,
        out_specs=[VMEM] * near,
        out_shape=[out] * near,
        compiler_params=params(FULL),
        cost_estimate=cost(4 * near * capacity * tokens * width, 4 << 20),
        name="dispatch_rows",
    )(facts, hot, rows, crossed, away)


def combine_kernel(near, capacity, facts_ref, hot_ref, *refs):
    blocks = refs[:near]
    outs = refs[near : near + 4]
    gathered, sems = refs[near + 4 :]
    plane = facts_ref[0]
    width = gathered.shape[2]

    def copies(which):
        return [
            pltpu.make_async_copy(
                block.at[pl.ds(which * capacity, capacity)],
                gathered.at[which, pl.ds(j * capacity, capacity)],
                sems.at[which, j],
            )
            for j, block in enumerate(blocks)
        ]

    pending = [copies(0), copies(1)]
    for which in (1, 0):
        for copy in pending[which]:
            copy.start()
    for which in (1, 0):
        for copy in pending[which]:
            copy.wait()
        own_ref, away_ref = outs[2 * which : 2 * which + 2]
        for own, out_ref in ((True, own_ref), (False, away_ref)):
            columns = columns_of(plane, width, own)
            out_ref[...] = dot(hot_ref[which], gathered[which, :, columns], 0, 0).astype(
                out_ref.dtype
            )


def combine_rows(facts, hot, blocks, capacity):
    near = len(blocks)
    tokens, width = hot.shape[2], blocks[0].shape[1]
    own = jax.ShapeDtypeStruct((tokens, width // 2), jnp.float32)
    away = jax.ShapeDtypeStruct((tokens, width // 2), jnp.bfloat16)
    return pl.pallas_call(
        functools.partial(combine_kernel, near, capacity),
        in_specs=[SMEM, VMEM] + [ANY] * near,
        out_specs=[VMEM] * 4,
        out_shape=[own, away, own, away],
        scratch_shapes=[
            pltpu.VMEM((2, near * capacity, width), jnp.bfloat16),
            pltpu.SemaphoreType.DMA((2, near)),
        ],
        compiler_params=params(FULL),
        cost_estimate=cost(4 * near * capacity * tokens * width, 4 << 20),
        name="combine_rows",
    )(facts, hot, *blocks)


def expert_kernel(near, facts_ref, weights_ref, router_ref, *refs):
    row_blocks, cot_blocks = refs[:near], refs[near : 2 * near]
    refs = refs[2 * near :]
    back_blocks, moe_blocks = refs[:near], refs[near : 2 * near]
    rows_ref, hidden_ref, gate_grad_ref, up_grad_ref, slot_grad_ref, logits_ref = refs[
        2 * near : 2 * near + 6
    ]
    cot_all, back_all, moe_all, weights, in_sems, out_sems = refs[2 * near + 6 :]
    index = pl.program_id(0)
    steps = pl.num_programs(0)
    block = row_blocks[0].shape[0]
    step = hidden_ref.shape[0]
    per_step = step // block

    def loads(j):
        place = pl.ds(j * block, block)
        return (
            pltpu.make_async_copy(row_blocks[j], rows_ref.at[place], in_sems.at[0, j]),
            pltpu.make_async_copy(cot_blocks[j], cot_all.at[place], in_sems.at[1, j]),
        )

    def store(which, j):
        source, targets = ((back_all, back_blocks), (moe_all, moe_blocks))[which]
        place = pl.ds(j * block, block)
        return pltpu.make_async_copy(source.at[place], targets[j], out_sems.at[which, j])

    @pl.when(index == 0)
    def _():
        for j in range(near):
            for copy in loads(j):
                copy.start()

    for s in range(near // per_step):

        @pl.when(index == s)
        def _():
            for j in range(s * per_step, (s + 1) * per_step):
                for copy in loads(j):
                    copy.wait()

    here = pl.ds(pl.multiple_of(index * step, step), step)
    width = rows_ref.shape[1]
    expert_count = router_ref.shape[0]
    rows = rows_ref[here, :]
    cot = cot_all[here, :width].astype(jnp.float32)
    picked = cot_all[here, width : width + 128][:, :expert_count]
    router = router_ref[...]
    logits = jnp.where(picked.astype(jnp.float32) > 0.5, dot(rows, router, 1, 1), NEGATIVE)
    terms = jnp.exp(logits - jnp.max(logits, axis=1, keepdims=True))
    gates = terms / jnp.sum(terms, axis=1, keepdims=True)
    expert = 2 * facts_ref[1] + facts_ref[0]
    own = (lax.broadcasted_iota(jnp.int32, gates.shape, 1) == expert).astype(jnp.float32)
    gate = jnp.sum(gates * own, axis=1, keepdims=True)

    @pl.when(index == 0)
    def _():
        columns = weights_ref.shape[-1]
        for i in range(3):
            for f in range(2):
                weights[i, :, f * columns : (f + 1) * columns] = weights_ref[:, f, i].reshape(
                    width, columns
                )

    gate_pre = dot(rows, weights[0])
    up_pre = dot(rows, weights[1])
    sigma = 1.0 / (1.0 + jnp.exp(-gate_pre))
    hidden = (gate_pre * sigma * up_pre).astype(jnp.bfloat16)
    hidden_ref[...] = hidden
    out = dot(hidden, weights[2], 1, 1)
    gate_grad = jnp.sum(out * cot, axis=1, keepdims=True)
    moe_all[here, :] = (gate * out).astype(jnp.bfloat16)

    def start_stores(which):
        for s in range(near // per_step):

            @pl.when(index == s)
            def _():
                for j in range(s * per_step, (s + 1) * per_step):
                    store(which, j).start()

    start_stores(1)
    slot_grad = (gate * cot).astype(jnp.bfloat16)
    slot_grad_ref[...] = slot_grad
    logits_grad = gate_grad * gate * (own - gates)
    upper = logits_grad.astype(jnp.bfloat16)
    lower = (logits_grad - upper.astype(jnp.float32)).astype(jnp.bfloat16)
    logits_ref[0] = upper
    logits_ref[1] = lower
    hidden_grad = dot(slot_grad, weights[2])
    gate_pre_grad = hidden_grad * up_pre * sigma * (1.0 + gate_pre * (1.0 - sigma))
    gate_pre_grad = gate_pre_grad.astype(jnp.bfloat16)
    up_pre_grad = (hidden_grad * gate_pre * sigma).astype(jnp.bfloat16)
    gate_grad_ref[...] = gate_pre_grad
    up_grad_ref[...] = up_pre_grad
    back = dot(upper, router) + dot(lower, router)
    back = back + dot(gate_pre_grad, weights[0], 1, 1) + dot(up_pre_grad, weights[1], 1, 1)
    back_all[here, :] = back.astype(jnp.bfloat16)
    start_stores(0)

    @pl.when(index == steps - 1)
    def _():
        for j in range(near):
            store(0, j).wait()
            store(1, j).wait()


def run_expert(facts, row_blocks, cot_blocks, weights, router_t):
    near = len(row_blocks)
    block, width = row_blocks[0].shape
    count = near * block
    cot_width = cot_blocks[0].shape[1]
    hidden = 2 * weights.shape[-1]
    steps = 2
    step = count // steps
    bf16 = jnp.bfloat16
    row_block = lambda columns: pl.BlockSpec((step, columns), lambda i: (i, 0))
    whole = lambda value: pl.BlockSpec(value.shape, lambda i: (0,) * value.ndim)
    experts = router_t.shape[0]
    block_shape = jax.ShapeDtypeStruct((block, width), bf16)
    results = pl.pallas_call(
        functools.partial(expert_kernel, near),
        grid=(steps,),
        in_specs=[SMEM, whole(weights), whole(router_t)] + [ANY] * (2 * near),
        out_specs=[ANY] * (2 * near)
        + [
            pl.BlockSpec((count, width), lambda i: (0, 0)),
            row_block(hidden),
            row_block(hidden),
            row_block(hidden),
            row_block(width),
            pl.BlockSpec((2, step, experts), lambda i: (0, i, 0)),
        ],
        out_shape=[block_shape] * (2 * near)
        + [
            jax.ShapeDtypeStruct((count, width), bf16),
            jax.ShapeDtypeStruct((count, hidden), bf16),
            jax.ShapeDtypeStruct((count, hidden), bf16),
            jax.ShapeDtypeStruct((count, hidden), bf16),
            jax.ShapeDtypeStruct((count, width), bf16),
            jax.ShapeDtypeStruct((2, count, experts), bf16),
        ],
        scratch_shapes=[
            pltpu.VMEM((count, cot_width), bf16),
            pltpu.VMEM((count, width), bf16),
            pltpu.VMEM((count, width), bf16),
            pltpu.VMEM((3, width, hidden), bf16),
            pltpu.SemaphoreType.DMA((2, near)),
            pltpu.SemaphoreType.DMA((2, near)),
        ],
        compiler_params=params(FULL),
        cost_estimate=cost(12 * count * width * hidden, 16 << 20, count * hidden),
        name="expert_rows",
    )(facts, weights, router_t, *row_blocks, *cot_blocks)
    return results[:near], results[near : 2 * near], results[2 * near :]


def put_grad(piece, out_ref, place=()):
    blocks, planes, block_rows, columns = (
        out_ref.shape[0],
        out_ref.shape[1],
        out_ref.shape[-2],
        out_ref.shape[-1],
    )
    piece = piece.astype(jnp.bfloat16)
    for f in range(planes):
        out_ref[(slice(None), f) + place] = piece[:, f * columns : (f + 1) * columns].reshape(
            blocks, block_rows, columns
        )


def grads_kernel(
    rows_ref,
    hidden_ref,
    gate_grad_ref,
    up_grad_ref,
    slot_grad_ref,
    logits_ref,
    pair_ref,
    down_ref,
    router_ref,
):
    rows = rows_ref[...]
    put_grad(dot(slot_grad_ref[...], hidden_ref[...], 0, 0), down_ref)
    put_grad(dot(rows, gate_grad_ref[...], 0, 0), pair_ref, (0,))
    put_grad(dot(rows, up_grad_ref[...], 0, 0), pair_ref, (1,))
    router_ref[...] = dot(logits_ref[0], rows, 0, 0) + dot(logits_ref[1], rows, 0, 0)


def run_grads(rows, hidden, gate_grad, up_grad, slot_grad, logits, shape):
    count, width = rows.shape
    steps = 4
    step = width // steps
    experts = logits.shape[2]
    blocks, planes, tail = shape[0] // steps, shape[1], shape[2:]
    column = pl.BlockSpec((count, step), lambda i: (0, i))
    whole = lambda value: pl.BlockSpec(value.shape, lambda i: (0,) * value.ndim)
    return pl.pallas_call(
        grads_kernel,
        grid=(steps,),
        in_specs=[column, whole(hidden), whole(gate_grad), whole(up_grad), column, whole(logits)],
        out_specs=[
            pl.BlockSpec((blocks, planes, 2) + tail, lambda i: (i, 0, 0, 0, 0)),
            pl.BlockSpec((blocks, planes) + tail, lambda i: (i, 0, 0, 0)),
            pl.BlockSpec((experts, step), lambda i: (0, i)),
        ],
        out_shape=[
            jax.ShapeDtypeStruct(shape[:2] + (2,) + tail, jnp.bfloat16),
            jax.ShapeDtypeStruct(shape, jnp.bfloat16),
            jax.ShapeDtypeStruct((experts, width), jnp.float32),
        ],
        compiler_params=params(FULL),
        cost_estimate=cost(6 * count * math.prod(shape), 12 << 20),
        name="expert_grads",
    )(rows, hidden, gate_grad, up_grad, slot_grad, logits)


def tables_kernel(place_ref, placement_ref, lengths_ref, facts_ref, cos_ref, sin_ref):
    holder = lax.fori_loop(
        0,
        placement_ref.shape[0],
        lambda i, total: total + jnp.where(placement_ref[i] == place_ref[1], i, 0),
        jnp.int32(0),
    )
    facts_ref[0] = place_ref[0]
    facts_ref[1] = place_ref[2]
    rows, lanes = cos_ref.shape
    row = lax.broadcasted_iota(jnp.int32, (rows, lanes), 0)
    start = jnp.zeros((rows, lanes), jnp.int32)
    end = jnp.int32(0)
    count = lengths_ref.shape[0]
    for j in range(count):
        end = end + lengths_ref[j, holder]
        facts_ref[3 + j] = end
        start = jnp.where(row >= end, end, start)
    facts_ref[2] = end
    half = HEAD_DIM // 2
    lane = lax.broadcasted_iota(jnp.int32, (rows, lanes), 1)
    index = jnp.bitwise_and(lane, half - 1).astype(jnp.float32)
    frequency = jnp.exp(-(2.0 * index / (2.0 * half)) * math.log(ROPE_BASE))
    angles = (row - start).astype(jnp.float32) * frequency
    cos_ref[...] = jnp.cos(angles)
    sine = jnp.sin(angles)
    sin_ref[...] = jnp.where(jnp.bitwise_and(lane, half) == 0, -sine, sine)


def make_tables(place, placement, lengths_t, rows):
    table = jax.ShapeDtypeStruct((rows, 128), jnp.float32)
    return pl.pallas_call(
        tables_kernel,
        in_specs=[SMEM, SMEM, SMEM],
        out_specs=[SMEM, VMEM, VMEM],
        out_shape=[
            jax.ShapeDtypeStruct((3 + lengths_t.shape[0],), jnp.int32),
            table,
            table,
        ],
        compiler_params=params(FULL),
        cost_estimate=cost(1 << 20, 1 << 18, rows * 256),
        name="tables",
    )(place, placement, lengths_t)


def turn(values, cos, sine):
    half = HEAD_DIM // 2
    lane = lax.broadcasted_iota(jnp.int32, cos.shape, 1)
    first = jnp.bitwise_and(lane, half) == 0
    pieces = []
    for c in range(values.shape[1] // 128):
        piece = values[:, c * 128 : (c + 1) * 128]
        other = jnp.where(first, pltpu.roll(piece, 128 - half, 1), pltpu.roll(piece, half, 1))
        pieces.append(piece * cos + other * sine)
    return jnp.concatenate(pieces, axis=1)


def allowed_pairs(facts_ref, rows):
    query = lax.broadcasted_iota(jnp.int32, (rows, rows), 0)
    key = lax.broadcasted_iota(jnp.int32, (rows, rows), 1)
    start = jnp.zeros((rows, rows), jnp.int32)
    for j in range(3, facts_ref.shape[0]):
        start = jnp.where(query >= facts_ref[j], facts_ref[j], start)
    return (key <= query) & (key >= start)


def pair_heads(values, g):
    chunk = values[:, 2 * g * HEAD_DIM : 2 * (g + 1) * HEAD_DIM]
    return jnp.concatenate([chunk[:, :HEAD_DIM], chunk[:, HEAD_DIM:]], axis=0)


def unpair_heads(values):
    rows = values.shape[0] // 2
    return jnp.concatenate([values[:rows], values[rows:]], axis=1)


def pair_scores(query, key, allowed):
    scores = dot(query, key, 1, 1) * (1.0 / HEAD_DIM)
    return jnp.where(jnp.concatenate([allowed, allowed], axis=0), scores, NEGATIVE)


def put_halves(ref, plane, own, away):
    width = ref.shape[1]
    ref[:, columns_of(plane, width, True)] = own
    ref[:, columns_of(plane, width, False)] = away


def inverse_norm(values):
    mean = jnp.mean(values * values, axis=1, keepdims=True)
    return lax.rsqrt(mean + EPSILON)


def attend_kernel(
    facts_ref,
    own_ref,
    away_ref,
    gain_ref,
    query_w_ref,
    key_w_ref,
    value_w_ref,
    output_w_ref,
    cos_ref,
    sin_ref,
    part_ref,
    normed_ref,
    query_ref,
    key_ref,
    value_ref,
    context_ref,
    total_ref,
    wide,
):
    put_halves(
        wide, facts_ref[0], own_ref[...].astype(jnp.float32), away_ref[...].astype(jnp.float32)
    )
    values = wide[...]
    rows = values.shape[0]
    normed = (values * inverse_norm(values) * gain_ref[...]).astype(jnp.bfloat16)
    normed_ref[...] = normed
    cos, sine = cos_ref[...], sin_ref[...]
    query = turn(dot(normed, query_w_ref[...]), cos, sine).astype(jnp.bfloat16)
    key = turn(dot(normed, key_w_ref[...]), cos, sine).astype(jnp.bfloat16)
    value = dot(normed, value_w_ref[...]).astype(jnp.bfloat16)
    query_ref[...] = query
    key_ref[...] = key
    value_ref[...] = value
    allowed = allowed_pairs(facts_ref, rows)
    live = lax.broadcasted_iota(jnp.int32, (rows, 2 * HEAD_DIM), 0) < facts_ref[2]
    pieces, totals = [], []
    for g in range(key.shape[1] // HEAD_DIM):
        place = slice(g * HEAD_DIM, (g + 1) * HEAD_DIM)
        scores = pair_scores(pair_heads(query, g), key[:, place], allowed)
        top = jnp.max(scores, axis=1, keepdims=True)
        terms = jnp.exp(scores - top)
        total = jnp.sum(terms, axis=1, keepdims=True)
        probs = (terms / total).astype(jnp.bfloat16)
        context = unpair_heads(dot(probs, value[:, place]))
        pieces.append(jnp.where(live, context, 0.0).astype(jnp.bfloat16))
        log_total = top + jnp.log(total)
        totals += [log_total[:rows], log_total[rows:]]
    context = jnp.concatenate(pieces, axis=1)
    context_ref[...] = context
    lane = lax.broadcasted_iota(jnp.int32, (rows, 128), 1)
    packed = jnp.zeros((rows, 128), jnp.float32)
    for h, log_total in enumerate(totals):
        packed = jnp.where(lane == h, log_total, packed)
    total_ref[...] = packed
    part_ref[...] = dot(context, output_w_ref[...]).astype(jnp.bfloat16)


def attend(facts, own, away, gain, query_w, key_w, value_w, output_w, cos, sine):
    rows = own.shape[0]
    width = 2 * own.shape[1]
    low = lambda columns: jax.ShapeDtypeStruct((rows, columns), jnp.bfloat16)
    return pl.pallas_call(
        attend_kernel,
        in_specs=[SMEM] + [VMEM] * 9,
        out_specs=[VMEM] * 7,
        out_shape=[
            low(width),
            low(width),
            low(query_w.shape[1]),
            low(key_w.shape[1]),
            low(value_w.shape[1]),
            low(query_w.shape[1]),
            jax.ShapeDtypeStruct((rows, 128), jnp.float32),
        ],
        scratch_shapes=[pltpu.VMEM((rows, width), jnp.float32)],
        compiler_params=params(FULL),
        cost_estimate=cost(8 * rows * width * width // 2, 8 << 20, rows * rows * 8),
        name="attend",
    )(facts, own, away, gain, query_w, key_w, value_w, output_w, cos, sine)


def mix_kernel(
    facts_ref, own_ref, away_ref, part_ref, recv_ref, gain_ref, residual_ref, mixed_ref, half_ref
):
    plane = facts_ref[0]
    put_halves(
        residual_ref, plane, own_ref[...].astype(jnp.float32), away_ref[...].astype(jnp.float32)
    )
    residual = residual_ref[...] + (
        part_ref[...].astype(jnp.float32) + recv_ref[...].astype(jnp.float32)
    )
    residual_ref[...] = residual
    mixed_ref[...] = (residual * inverse_norm(residual) * gain_ref[...]).astype(jnp.bfloat16)
    half_ref[...] = mixed_ref[:, columns_of(plane, residual.shape[1], True)]


def mix(facts, own, away, part, recv, gain):
    rows, width = part.shape
    return pl.pallas_call(
        mix_kernel,
        in_specs=[SMEM] + [VMEM] * 5,
        out_specs=[VMEM] * 3,
        out_shape=[
            jax.ShapeDtypeStruct((rows, width), jnp.float32),
            jax.ShapeDtypeStruct((rows, width), jnp.bfloat16),
            jax.ShapeDtypeStruct((rows, width // 2), jnp.bfloat16),
        ],
        compiler_params=params(FULL),
        cost_estimate=cost(rows * width * 8, 3 << 20),
        name="mix",
    )(facts, own, away, part, recv, gain)


def attend_back_kernel(
    facts_ref,
    mixed_ref,
    mixed_away_ref,
    cot_ref,
    cot_away_ref,
    residual_ref,
    own_ref,
    away_ref,
    gain_ref,
    expert_gain_ref,
    normed_ref,
    query_ref,
    key_ref,
    value_ref,
    context_ref,
    total_ref,
    query_w_ref,
    key_w_ref,
    value_w_ref,
    output_w_ref,
    cos_ref,
    sin_ref,
    router_ref,
    parts_ref,
    normed_own_ref,
    normed_away_ref,
    base_ref,
    inner_ref,
    wide,
):
    plane = facts_ref[0]
    own_columns = columns_of(plane, wide.shape[1], True)
    away_columns = columns_of(plane, wide.shape[1], False)
    rows, width = wide.shape

    put_halves(
        wide, plane, mixed_ref[...].astype(jnp.float32), mixed_away_ref[...].astype(jnp.float32)
    )
    mixed_grad = wide[...]
    put_halves(
        wide, plane, cot_ref[...].astype(jnp.float32), cot_away_ref[...].astype(jnp.float32)
    )
    residual = residual_ref[...]
    inverse = inverse_norm(residual)
    scaled = mixed_grad * expert_gain_ref[...]
    mean = jnp.mean(scaled * residual, axis=1, keepdims=True)
    residual_grad = (
        wide[...] + inverse * scaled - residual * (inverse * inverse * inverse * mean)
    )
    expert_gain_grad = 0.5 * jnp.sum(mixed_grad * residual * inverse, axis=0, keepdims=True)
    wide[...] = residual_grad
    base_ref[...] = wide[:, own_columns]
    low = residual_grad.astype(jnp.bfloat16)
    context = context_ref[...]
    columns = context.shape[1]
    parts_ref[:, :columns] = dot(low, context, 0, 0).astype(parts_ref.dtype)
    live = lax.broadcasted_iota(jnp.int32, (rows, columns), 0) < facts_ref[2]
    context_grad = jnp.where(live, dot(low, output_w_ref[...], 1, 1), 0.0).astype(jnp.bfloat16)

    query, key, value = query_ref[...], key_ref[...], value_ref[...]
    totals = total_ref[...]
    allowed = allowed_pairs(facts_ref, rows)
    scale = 1.0 / HEAD_DIM
    query_grads, key_grads, value_grads = [], [], []
    for g in range(key.shape[1] // HEAD_DIM):
        place = slice(g * HEAD_DIM, (g + 1) * HEAD_DIM)
        pair = pair_heads(query, g)
        pair_grad = pair_heads(context_grad, g)
        total = jnp.concatenate([totals[:, 2 * g : 2 * g + 1], totals[:, 2 * g + 1 : 2 * g + 2]])
        probs = jnp.exp(pair_scores(pair, key[:, place], allowed) - total)
        prob_grad = dot(pair_grad, value[:, place], 1, 1)
        inner = jnp.sum(probs * prob_grad, axis=1, keepdims=True)
        score_grad = (probs * (prob_grad - inner)).astype(jnp.bfloat16)
        query_grads.append(unpair_heads(dot(score_grad, key[:, place]) * scale))
        key_grads.append(dot(score_grad, pair, 0, 0) * scale)
        value_grads.append(dot(probs.astype(jnp.bfloat16), pair_grad, 0, 0))
    cos, sine = cos_ref[...], -sin_ref[...]
    query_grad = turn(jnp.concatenate(query_grads, axis=1), cos, sine).astype(jnp.bfloat16)
    key_grad = turn(jnp.concatenate(key_grads, axis=1), cos, sine).astype(jnp.bfloat16)
    value_grad = jnp.concatenate(value_grads, axis=1).astype(jnp.bfloat16)
    normed_t = normed_ref[...]
    start = columns
    for grad in (query_grad, key_grad, value_grad):
        size = grad.shape[1]
        parts_ref[:, start : start + size] = dot(normed_t, grad, 0, 0).astype(parts_ref.dtype)
        start += size
    normed_grad = (
        dot(query_grad, query_w_ref[...], 1, 1)
        + dot(key_grad, key_w_ref[...], 1, 1)
        + dot(value_grad, value_w_ref[...], 1, 1)
    )
    put_halves(
        wide, plane, own_ref[...].astype(jnp.float32), away_ref[...].astype(jnp.float32)
    )
    values = wide[...]
    product = normed_grad * values
    gain_grad = jnp.sum(product * inverse_norm(values), axis=0, keepdims=True)
    inner = jnp.sum(product * gain_ref[...], axis=1, keepdims=True)
    inner_ref[...] = jnp.broadcast_to(inner, (rows, 128)).T[: inner_ref.shape[0]]
    wide[...] = normed_grad
    normed_own_ref[...] = wide[:, own_columns]
    normed_away_ref[...] = wide[:, away_columns].astype(jnp.bfloat16)
    experts = router_ref.shape[0]
    rest = jnp.zeros((128 - experts - 2, width), jnp.float32)
    packed = jnp.concatenate([router_ref[...], gain_grad, expert_gain_grad, rest], axis=0)
    parts_ref[:, start : start + 128] = packed.T.astype(parts_ref.dtype)


def attend_back(facts, *values):
    mixed, query_w, key_w, value_w = values[0], values[15], values[16], values[17]
    rows, half = mixed.shape
    width = 2 * half
    columns = 2 * query_w.shape[1] + key_w.shape[1] + value_w.shape[1] + 128
    wide = lambda columns, kind: jax.ShapeDtypeStruct((rows, columns), kind)
    return pl.pallas_call(
        attend_back_kernel,
        in_specs=[SMEM] + [VMEM] * len(values),
        out_specs=[VMEM] * 5,
        out_shape=[
            jax.ShapeDtypeStruct((width, columns), jnp.bfloat16),
            wide(half, jnp.float32),
            wide(half, jnp.bfloat16),
            wide(half, jnp.float32),
            jax.ShapeDtypeStruct((8, rows), jnp.float32),
        ],
        scratch_shapes=[pltpu.VMEM((rows, width), jnp.float32)],
        compiler_params=params(FULL),
        cost_estimate=cost(16 * rows * width * half * 2, 14 << 20, rows * rows * 8),
        name="attend_back",
    )(facts, *values)


def finish_kernel(
    facts_ref,
    own_ref,
    away_ref,
    gain_ref,
    residual_ref,
    moe_ref,
    moe_recv_ref,
    moe_cross_ref,
    base_ref,
    normed_ref,
    normed_recv_ref,
    inner_ref,
    inner_recv_ref,
    out_ref,
):
    rows, half = own_ref.shape
    own_columns = columns_of(facts_ref[0], 2 * half, True)
    own = own_ref[...].astype(jnp.float32)
    away = away_ref[...].astype(jnp.float32)
    total = jnp.sum(own * own, axis=1, keepdims=True) + jnp.sum(away * away, axis=1, keepdims=True)
    inverse = lax.rsqrt(total / (2 * half) + EPSILON)
    inner = (inner_ref[0:1, :] + inner_recv_ref[0:1, :]) / (2 * half)
    inner = jnp.broadcast_to(inner, (128, rows)).T[:, :1]
    normed = normed_ref[...] + normed_recv_ref[...].astype(jnp.float32)
    grad = (
        base_ref[...]
        + inverse * normed * gain_ref[:, own_columns]
        - own * (inverse * inverse * inverse * inner)
    )
    moe = (
        moe_ref[...]
        + moe_recv_ref[...].astype(jnp.float32)
        + moe_cross_ref[...].astype(jnp.float32)
    )
    out_ref[:, :half] = (residual_ref[:, own_columns] + moe).astype(out_ref.dtype)
    out_ref[:, half:] = grad.astype(out_ref.dtype)


def finish(facts, *values):
    rows, half = values[0].shape
    return pl.pallas_call(
        finish_kernel,
        in_specs=[SMEM] + [VMEM] * len(values),
        out_specs=VMEM,
        out_shape=jax.ShapeDtypeStruct((rows, 2 * half), jnp.bfloat16),
        compiler_params=params(FULL),
        cost_estimate=cost(rows * half * 16, 4 << 20),
        name="finish",
    )(facts, *values)


def local(
    inputs,
    cotangent,
    attn_gain,
    expert_gain,
    query_weight,
    key_weight,
    value_weight,
    output_weight,
    router_weight,
    gate_weight,
    up_weight,
    down_weight,
    routes,
    lengths,
    placement,
):
    row_count, top_count = routes.shape
    expert_count = router_weight.shape[1]
    capacity = row_count * top_count // expert_count
    kv_local = key_weight.shape[1] // HEAD_DIM
    heads_local = query_weight.shape[1] // HEAD_DIM
    group = heads_local // kv_local
    scale = 1.0 / HEAD_DIM
    width_half = inputs.shape[1]
    width = 2 * width_half
    plane = lax.axis_index("tensor")
    devices = lax.axis_size("dp")
    dp_index = lax.axis_index("dp")
    members = expert_count // 2
    near = members // 2
    clusters = devices // members
    member = dp_index % members
    expert = 2 * member + plane
    inside = [[c * members + m for m in range(members)] for c in range(clusters)]
    across = [[c * members + m for c in range(clusters)] for m in range(members)]

    def cross(values):
        return lax.ppermute(values, "dp", [(i, i ^ near) for i in range(devices)])

    def spread(blocks):
        return [blocks[0]] + [
            lax.ppermute(blocks[s], "dp", [(i, i ^ s) for i in range(devices)])
            for s in range(1, near)
        ]

    def halves(values, axis):
        size = values.shape[axis] // 2
        return (
            lax.dynamic_slice_in_dim(values, plane * size, size, axis),
            lax.dynamic_slice_in_dim(values, (1 - plane) * size, size, axis),
        )

    def join(own, other, axis):
        first = jnp.where(plane == 0, own, other)
        second = jnp.where(plane == 0, other, own)
        return jnp.concatenate([first, second], axis=axis)

    def add_planes(part):
        low = part.astype(jnp.bfloat16)
        return low.astype(jnp.float32) + swap_tensor(low).astype(jnp.float32)

    routes_t = routes.T
    away = swap_tensor(inputs)
    partner_t = cross(routes_t)
    cot_cross = cross(cotangent)
    cot_away = swap_tensor(cotangent)
    cot_cross_away = swap_tensor(cot_cross)
    place = jnp.stack([plane, dp_index, member]).astype(jnp.int32)
    facts, cos_table, sin_table = make_tables(place, placement, lengths.T, row_count)
    gain_one, gain_two = attn_gain[None], expert_gain[None]
    attn_part, normed, query, key, value, context, log_total = attend(
        facts,
        inputs,
        away,
        gain_one,
        query_weight,
        key_weight,
        value_weight,
        output_weight,
        cos_table,
        sin_table,
    )

    def to_owner(values):
        if clusters == 1:
            owned = lax.all_to_all(
                values, ("dp", "tensor"), split_axis=0, concat_axis=0, tiled=True
            )
            return owned.reshape((devices, 2) + owned.shape[1:])
        by_plane = values.reshape((members, 2) + values.shape[1:])
        own_w = lax.dynamic_index_in_dim(by_plane, plane, 1, keepdims=False)
        other_w = swap_tensor(lax.dynamic_index_in_dim(by_plane, 1 - plane, 1, keepdims=False))
        owned = jnp.stack(
            [jnp.where(plane == 0, own_w, other_w), jnp.where(plane == 0, other_w, own_w)], axis=1
        )
        owned = lax.all_to_all(
            owned, "dp", split_axis=0, concat_axis=0, tiled=True, axis_index_groups=inside
        )
        owned = lax.all_gather(owned, "dp", axis=0, tiled=True, axis_index_groups=across)
        owned = owned.reshape((members, clusters) + owned.shape[1:])
        owned = jnp.moveaxis(owned, 1, -3)
        return owned.reshape(owned.shape[:-3] + (-1, owned.shape[-1]))

    def from_owner(values):
        if clusters == 1:
            return lax.all_to_all(
                values.reshape((2 * devices,) + values.shape[2:]),
                ("dp", "tensor"),
                split_axis=0,
                concat_axis=0,
                tiled=True,
            )
        values = values.reshape(values.shape[:-2] + (clusters, -1, values.shape[-1]))
        values = jnp.moveaxis(values, -3, 1)
        values = values.reshape((devices,) + values.shape[2:])
        values = lax.psum_scatter(
            values, "dp", scatter_dimension=0, tiled=True, axis_index_groups=across
        )
        values = lax.all_to_all(
            values, "dp", split_axis=0, concat_axis=0, tiled=True, axis_index_groups=inside
        )
        own_g = lax.dynamic_index_in_dim(values, plane, 1, keepdims=False)
        other_g = swap_tensor(lax.dynamic_index_in_dim(values, 1 - plane, 1, keepdims=False))
        values = jnp.stack(
            [jnp.where(plane == 0, own_g, other_g), jnp.where(plane == 0, other_g, own_g)], axis=1
        )
        return values.reshape((expert_count,) + values.shape[2:])

    owned = to_owner(
        after(
            jnp.stack([gate_weight, up_weight, jnp.swapaxes(down_weight, 1, 2)], axis=1),
            away,
            partner_t,
            cot_away,
            cot_cross,
        )
    )

    hot, cot_blocks = dispatch_cot(
        facts,
        routes_t,
        partner_t,
        cotangent,
        cot_cross,
        cot_away,
        cot_cross_away,
        near,
        capacity,
        expert_count,
    )
    cot_blocks = spread(cot_blocks)

    def combine(hot, blocks):
        mine, mine_away, others, others_away = combine_rows(facts, hot, blocks, capacity)
        others = others + swap_tensor(others_away).astype(jnp.float32)
        return mine, swap_tensor(mine_away), cross(others.astype(jnp.bfloat16))

    residual, mixed_rows, mixed_half = mix(
        facts, inputs, away, attn_part, swap_tensor(attn_part), gain_two
    )
    mixed_cross = cross(mixed_half)
    mixed_away = swap_tensor(mixed_cross)
    row_blocks = spread(
        dispatch_rows(
            facts, after(hot, *cot_blocks[1:7]), mixed_rows, mixed_cross, mixed_away, near, capacity
        )
    )

    back_blocks, moe_blocks, kept = run_expert(
        facts, row_blocks, cot_blocks, owned, router_weight.T
    )
    back_blocks = spread(back_blocks)
    pair_part, down_part, router_part = run_grads(
        *kept, (members, 2, width // members, gate_weight.shape[2])
    )
    down_share = from_owner(down_part)
    moe_blocks = spread(moe_blocks)
    mine, mine_recv, mine_cross = combine(after(hot, down_share), back_blocks)
    mixed_half = mine + mine_recv.astype(jnp.float32) + mine_cross.astype(jnp.float32)
    mixed_half = mixed_half.astype(jnp.bfloat16)
    mixed_away = swap_tensor(mixed_half)
    pair_share = from_owner(after(pair_part, mixed_half))
    moe_parts = combine(hot, moe_blocks)

    parts, normed_own, normed_away, base_half, inner = attend_back(
        facts,
        mixed_half,
        mixed_away,
        cotangent,
        cot_away,
        after(residual, *moe_blocks),
        inputs,
        away,
        gain_one,
        gain_two,
        normed,
        query,
        key,
        value,
        context,
        log_total,
        query_weight,
        key_weight,
        value_weight,
        output_weight,
        cos_table,
        sin_table,
        router_part,
    )
    share = lax.psum_scatter(parts, "dp", scatter_dimension=0, tiled=True)
    cuts = [context.shape[1]]
    for w in (query_weight, key_weight, value_weight):
        cuts.append(cuts[-1] + w.shape[1])
    small = share[:, cuts[3] :]
    small = small.astype(jnp.float32) + swap_tensor(small).astype(jnp.float32)
    share = share.astype(jnp.float32)
    output_part = share[:, : cuts[0]].T
    query_part = share[:, cuts[0] : cuts[1]]
    key_part = share[:, cuts[1] : cuts[2]]
    value_part = share[:, cuts[2] : cuts[3]]
    router_share = small[:, :expert_count]
    attn_gain_part = small[:, expert_count]
    expert_gain_part = small[:, expert_count + 1]

    gate_w_part = pair_share[:, 0].astype(jnp.float32)
    up_w_part = pair_share[:, 1].astype(jnp.float32)
    down_w_part = jnp.swapaxes(down_share, 1, 2).astype(jnp.float32)

    piece_rows = row_count // devices
    moved = finish(
        facts,
        inputs,
        away,
        gain_one,
        residual,
        *moe_parts,
        base_half,
        normed_own,
        swap_tensor(normed_away),
        inner,
        swap_tensor(inner),
    )
    moved = after(moved, pair_share)
    moved = lax.all_to_all(
        moved.reshape(devices, piece_rows, width), "dp", split_axis=0, concat_axis=0, tiled=True
    )
    moved = jnp.take(moved, placement, axis=0)
    moved = lax.all_to_all(moved, "dp", split_axis=0, concat_axis=0, tiled=True)
    moved = moved.reshape(row_count, width)
    outputs = moved[:, :width_half]
    input_result = moved[:, width_half:].astype(jnp.float32)
    return (
        outputs,
        input_result,
        attn_gain_part,
        expert_gain_part,
        query_part,
        key_part,
        value_part,
        output_part,
        router_share,
        gate_w_part,
        up_w_part,
        down_w_part,
    )


def solution(mesh):
    in_specs = (
        P("dp", "tensor"),
        P("dp", "tensor"),
        P(),
        P(),
        P(None, "tensor"),
        P(None, "tensor"),
        P(None, "tensor"),
        P("tensor", None),
        P(),
        P(None, "dp", "tensor"),
        P(None, "dp", "tensor"),
        P(None, "tensor", "dp"),
        P("dp", None),
        P(),
        P(),
    )
    out_specs = (
        P("dp", "tensor"),
        P("dp", "tensor"),
        P("dp"),
        P("dp"),
        P("dp", "tensor"),
        P("dp", "tensor"),
        P("dp", "tensor"),
        P("tensor", "dp"),
        P("dp", None),
        P(None, "dp", "tensor"),
        P(None, "dp", "tensor"),
        P(None, "tensor", "dp"),
    )
    return jax.shard_map(local, mesh=mesh, in_specs=in_specs, out_specs=out_specs, check_vma=False)
```

```python
import functools
import math

import jax
import jax.numpy as jnp
from jax import lax
from jax.experimental import pallas as pl
from jax.experimental.pallas import tpu as pltpu
from jax.sharding import PartitionSpec as P

HEAD_DIM = 64


EPSILON = 1e-06
ROPE_BASE = 10000.0
NEGATIVE = -1e30


def swap_tensor(values):
    return lax.ppermute(values, "tensor", [(0, 1), (1, 0)])


def mm(left, right, contract):
    return lax.dot_general(
        left, right, ((contract[:1], contract[1:]), ((), ())), preferred_element_type=jnp.float32
    )


def after(values, *others):
    return lax.optimization_barrier((values,) + others)[0]


def dot(left, right, left_axis=1, right_axis=0):
    return lax.dot_general(
        left,
        right,
        (((left_axis,), (right_axis,)), ((), ())),
        preferred_element_type=jnp.float32,
    )


def params(megabytes):
    return pltpu.CompilerParams(vmem_limit_bytes=megabytes << 20)


def cost(flops, size, transcendentals=0):
    return pl.CostEstimate(
        flops=flops, bytes_accessed=size, transcendentals=transcendentals
    )


SMEM = pl.BlockSpec(memory_space=pltpu.SMEM)
VMEM = pl.BlockSpec(memory_space=pltpu.VMEM)
ANY = pl.BlockSpec(memory_space=pl.ANY)
FULL = 60


def columns_of(plane, width, own):
    half = width // 2
    start = plane * half if own else (1 - plane) * half
    return pl.ds(pl.multiple_of(start, half), half)


def write_blocks(product, columns, out_refs, capacity, which):
    for j, out_ref in enumerate(out_refs):
        out_ref[which * capacity : (which + 1) * capacity, columns] = product[
            j * capacity : (j + 1) * capacity
        ].astype(out_ref.dtype)


def dispatch_cot_kernel(capacity, expert_count, facts_ref, routes_ref, partner_ref, *refs):
    own_ref, cross_ref, away_ref, cross_away_ref, hot_ref = refs[:5]
    out_refs = refs[5:]
    plane, member, live_count = facts_ref[0], facts_ref[1], facts_ref[2]
    tokens = routes_ref.shape[1]
    near = len(out_refs)
    width = 2 * own_ref.shape[1]
    row = lax.broadcasted_iota(jnp.int32, (tokens, tokens), 0)
    column = lax.broadcasted_iota(jnp.int32, (tokens, tokens), 1)
    before = jnp.where(row < column, 1.0, 0.0).astype(jnp.bfloat16)
    live = lax.broadcasted_iota(jnp.int32, (1, tokens), 1) < live_count
    names = lax.broadcasted_iota(jnp.int32, (128, tokens), 0)
    slots = lax.broadcasted_iota(jnp.int32, (near, capacity, tokens), 1)
    ids = lax.broadcasted_iota(jnp.int32, (near, tokens), 0)
    near_experts = 2 * jnp.bitwise_xor(ids, member) + plane
    values = (
        (own_ref[...], away_ref[...]),
        (cross_ref[...], cross_away_ref[...]),
    )
    for which, source in enumerate((routes_ref, partner_ref)):
        picked = names < 0
        counted = ids < 0
        for k in range(source.shape[0]):
            route = source[k : k + 1, :]
            picked = picked | (names == route)
            counted = counted | (near_experts == route)
        counted = counted & live
        place = dot(jnp.where(counted, 1.0, 0.0).astype(jnp.bfloat16), before)
        place = jnp.where(counted, place.astype(jnp.int32), -1)
        hot = jnp.where(place[:, None, :] == slots, 1.0, 0.0).astype(jnp.bfloat16)
        hot = hot.reshape(near * capacity, tokens)
        hot_ref[which] = hot
        own, away = values[which]
        write_blocks(dot(hot, own), columns_of(plane, width, True), out_refs, capacity, which)
        write_blocks(dot(hot, away), columns_of(plane, width, False), out_refs, capacity, which)
        picked = jnp.where(picked, 1.0, 0.0).astype(jnp.bfloat16)
        write_blocks(
            dot(hot, picked, 1, 1), slice(width, width + 128), out_refs, capacity, which
        )


def dispatch_cot(
    facts, routes_t, partner_t, own, crossed, away, cross_away, near, capacity, expert_count
):
    tokens, half = own.shape
    out = jax.ShapeDtypeStruct((2 * capacity, 2 * half + 128), jnp.bfloat16)
    hot = jax.ShapeDtypeStruct((2, near * capacity, tokens), jnp.bfloat16)
    results = pl.pallas_call(
        functools.partial(dispatch_cot_kernel, capacity, expert_count),
        in_specs=[SMEM] + [VMEM] * 6,
        out_specs=[VMEM] * (1 + near),
        out_shape=[hot] + [out] * near,
        compiler_params=params(FULL),
        cost_estimate=cost(8 * near * capacity * tokens * half, 4 << 20),
        name="dispatch_cot",
    )(facts, routes_t, partner_t, own, crossed, away, cross_away)
    return results[0], results[1:]


def dispatch_rows_kernel(capacity, facts_ref, hot_ref, rows_ref, cross_ref, away_ref, *out_refs):
    plane = facts_ref[0]
    width = rows_ref.shape[1]
    write_blocks(dot(hot_ref[0], rows_ref[...]), slice(0, width), out_refs, capacity, 0)
    own, away = columns_of(plane, width, True), columns_of(plane, width, False)
    write_blocks(dot(hot_ref[1], cross_ref[...]), own, out_refs, capacity, 1)
    write_blocks(dot(hot_ref[1], away_ref[...]), away, out_refs, capacity, 1)


def dispatch_rows(facts, hot, rows, crossed, away, near, capacity):
    tokens, width = rows.shape
    out = jax.ShapeDtypeStruct((2 * capacity, width), jnp.bfloat16)
    return pl.pallas_call(
        functools.partial(dispatch_rows_kernel, capacity),
        in_specs=[SMEM] + [VMEM] * 4,
        out_specs=[VMEM] * near,
        out_shape=[out] * near,
        compiler_params=params(FULL),
        cost_estimate=cost(4 * near * capacity * tokens * width, 4 << 20),
        name="dispatch_rows",
    )(facts, hot, rows, crossed, away)


def combine_kernel(near, capacity, facts_ref, hot_ref, *refs):
    blocks = refs[:near]
    outs = refs[near : near + 4]
    gathered, sems = refs[near + 4 :]
    plane = facts_ref[0]
    width = gathered.shape[2]

    def copies(which):
        return [
            pltpu.make_async_copy(
                block.at[pl.ds(which * capacity, capacity)],
                gathered.at[which, pl.ds(j * capacity, capacity)],
                sems.at[which, j],
            )
            for j, block in enumerate(blocks)
        ]

    pending = [copies(0), copies(1)]
    for which in (1, 0):
        for copy in pending[which]:
            copy.start()
    for which in (1, 0):
        for copy in pending[which]:
            copy.wait()
        own_ref, away_ref = outs[2 * which : 2 * which + 2]
        for own, out_ref in ((True, own_ref), (False, away_ref)):
            columns = columns_of(plane, width, own)
            out_ref[...] = dot(hot_ref[which], gathered[which, :, columns], 0, 0).astype(
                out_ref.dtype
            )


def combine_rows(facts, hot, blocks, capacity):
    near = len(blocks)
    tokens, width = hot.shape[2], blocks[0].shape[1]
    own = jax.ShapeDtypeStruct((tokens, width // 2), jnp.float32)
    away = jax.ShapeDtypeStruct((tokens, width // 2), jnp.bfloat16)
    return pl.pallas_call(
        functools.partial(combine_kernel, near, capacity),
        in_specs=[SMEM, VMEM] + [ANY] * near,
        out_specs=[VMEM] * 4,
        out_shape=[own, away, own, away],
        scratch_shapes=[
            pltpu.VMEM((2, near * capacity, width), jnp.bfloat16),
            pltpu.SemaphoreType.DMA((2, near)),
        ],
        compiler_params=params(FULL),
        cost_estimate=cost(4 * near * capacity * tokens * width, 4 << 20),
        name="combine_rows",
    )(facts, hot, *blocks)


def expert_kernel(near, facts_ref, weights_ref, router_ref, *refs):
    row_blocks, cot_blocks = refs[:near], refs[near : 2 * near]
    refs = refs[2 * near :]
    back_blocks, moe_blocks = refs[:near], refs[near : 2 * near]
    rows_ref, hidden_ref, gate_grad_ref, up_grad_ref, slot_grad_ref, logits_ref = refs[
        2 * near : 2 * near + 6
    ]
    cot_all, back_all, moe_all, weights, in_sems, out_sems = refs[2 * near + 6 :]
    index = pl.program_id(0)
    steps = pl.num_programs(0)
    block = row_blocks[0].shape[0]
    step = hidden_ref.shape[0]
    per_step = step // block

    def loads(j):
        place = pl.ds(j * block, block)
        return (
            pltpu.make_async_copy(row_blocks[j], rows_ref.at[place], in_sems.at[0, j]),
            pltpu.make_async_copy(cot_blocks[j], cot_all.at[place], in_sems.at[1, j]),
        )

    def store(which, j):
        source, targets = ((back_all, back_blocks), (moe_all, moe_blocks))[which]
        place = pl.ds(j * block, block)
        return pltpu.make_async_copy(source.at[place], targets[j], out_sems.at[which, j])

    @pl.when(index == 0)
    def _():
        for j in range(near):
            for copy in loads(j):
                copy.start()

    for s in range(near // per_step):

        @pl.when(index == s)
        def _():
            for j in range(s * per_step, (s + 1) * per_step):
                for copy in loads(j):
                    copy.wait()

    here = pl.ds(pl.multiple_of(index * step, step), step)
    width = rows_ref.shape[1]
    expert_count = router_ref.shape[0]
    rows = rows_ref[here, :]
    cot = cot_all[here, :width].astype(jnp.float32)
    picked = cot_all[here, width : width + 128][:, :expert_count]
    router = router_ref[...]
    logits = jnp.where(picked.astype(jnp.float32) > 0.5, dot(rows, router, 1, 1), NEGATIVE)
    terms = jnp.exp(logits - jnp.max(logits, axis=1, keepdims=True))
    gates = terms / jnp.sum(terms, axis=1, keepdims=True)
    expert = 2 * facts_ref[1] + facts_ref[0]
    own = (lax.broadcasted_iota(jnp.int32, gates.shape, 1) == expert).astype(jnp.float32)
    gate = jnp.sum(gates * own, axis=1, keepdims=True)

    @pl.when(index == 0)
    def _():
        columns = weights_ref.shape[-1]
        for i in range(3):
            for f in range(2):
                weights[i, :, f * columns : (f + 1) * columns] = weights_ref[:, f, i].reshape(
                    width, columns
                )

    gate_pre = dot(rows, weights[0])
    up_pre = dot(rows, weights[1])
    sigma = 1.0 / (1.0 + jnp.exp(-gate_pre))
    hidden = (gate_pre * sigma * up_pre).astype(jnp.bfloat16)
    hidden_ref[...] = hidden
    out = dot(hidden, weights[2], 1, 1)
    gate_grad = jnp.sum(out * cot, axis=1, keepdims=True)
    moe_all[here, :] = (gate * out).astype(jnp.bfloat16)

    def start_stores(which):
        for s in range(near // per_step):

            @pl.when(index == s)
            def _():
                for j in range(s * per_step, (s + 1) * per_step):
                    store(which, j).start()

    start_stores(1)
    slot_grad = (gate * cot).astype(jnp.bfloat16)
    slot_grad_ref[...] = slot_grad
    logits_grad = gate_grad * gate * (own - gates)
    upper = logits_grad.astype(jnp.bfloat16)
    lower = (logits_grad - upper.astype(jnp.float32)).astype(jnp.bfloat16)
    logits_ref[0] = upper
    logits_ref[1] = lower
    hidden_grad = dot(slot_grad, weights[2])
    gate_pre_grad = hidden_grad * up_pre * sigma * (1.0 + gate_pre * (1.0 - sigma))
    gate_pre_grad = gate_pre_grad.astype(jnp.bfloat16)
    up_pre_grad = (hidden_grad * gate_pre * sigma).astype(jnp.bfloat16)
    gate_grad_ref[...] = gate_pre_grad
    up_grad_ref[...] = up_pre_grad
    back = dot(upper, router) + dot(lower, router)
    back = back + dot(gate_pre_grad, weights[0], 1, 1) + dot(up_pre_grad, weights[1], 1, 1)
    back_all[here, :] = back.astype(jnp.bfloat16)
    start_stores(0)

    @pl.when(index == steps - 1)
    def _():
        for j in range(near):
            store(0, j).wait()
            store(1, j).wait()


def run_expert(facts, row_blocks, cot_blocks, weights, router_t):
    near = len(row_blocks)
    block, width = row_blocks[0].shape
    count = near * block
    cot_width = cot_blocks[0].shape[1]
    hidden = 2 * weights.shape[-1]
    steps = 2
    step = count // steps
    bf16 = jnp.bfloat16
    row_block = lambda columns: pl.BlockSpec((step, columns), lambda i: (i, 0))
    whole = lambda value: pl.BlockSpec(value.shape, lambda i: (0,) * value.ndim)
    experts = router_t.shape[0]
    block_shape = jax.ShapeDtypeStruct((block, width), bf16)
    results = pl.pallas_call(
        functools.partial(expert_kernel, near),
        grid=(steps,),
        in_specs=[SMEM, whole(weights), whole(router_t)] + [ANY] * (2 * near),
        out_specs=[ANY] * (2 * near)
        + [
            pl.BlockSpec((count, width), lambda i: (0, 0)),
            row_block(hidden),
            row_block(hidden),
            row_block(hidden),
            row_block(width),
            pl.BlockSpec((2, step, experts), lambda i: (0, i, 0)),
        ],
        out_shape=[block_shape] * (2 * near)
        + [
            jax.ShapeDtypeStruct((count, width), bf16),
            jax.ShapeDtypeStruct((count, hidden), bf16),
            jax.ShapeDtypeStruct((count, hidden), bf16),
            jax.ShapeDtypeStruct((count, hidden), bf16),
            jax.ShapeDtypeStruct((count, width), bf16),
            jax.ShapeDtypeStruct((2, count, experts), bf16),
        ],
        scratch_shapes=[
            pltpu.VMEM((count, cot_width), bf16),
            pltpu.VMEM((count, width), bf16),
            pltpu.VMEM((count, width), bf16),
            pltpu.VMEM((3, width, hidden), bf16),
            pltpu.SemaphoreType.DMA((2, near)),
            pltpu.SemaphoreType.DMA((2, near)),
        ],
        compiler_params=params(FULL),
        cost_estimate=cost(12 * count * width * hidden, 16 << 20, count * hidden),
        name="expert_rows",
    )(facts, weights, router_t, *row_blocks, *cot_blocks)
    return results[:near], results[near : 2 * near], results[2 * near :]


def put_grad(piece, out_ref, place=()):
    blocks, planes, block_rows, columns = (
        out_ref.shape[0],
        out_ref.shape[1],
        out_ref.shape[-2],
        out_ref.shape[-1],
    )
    piece = piece.astype(jnp.bfloat16)
    for f in range(planes):
        out_ref[(slice(None), f) + place] = piece[:, f * columns : (f + 1) * columns].reshape(
            blocks, block_rows, columns
        )


def grads_kernel(
    rows_ref,
    hidden_ref,
    gate_grad_ref,
    up_grad_ref,
    slot_grad_ref,
    logits_ref,
    pair_ref,
    down_ref,
    router_ref,
):
    rows = rows_ref[...]
    put_grad(dot(slot_grad_ref[...], hidden_ref[...], 0, 0), down_ref)
    put_grad(dot(rows, gate_grad_ref[...], 0, 0), pair_ref, (0,))
    put_grad(dot(rows, up_grad_ref[...], 0, 0), pair_ref, (1,))
    router_ref[...] = dot(logits_ref[0], rows, 0, 0) + dot(logits_ref[1], rows, 0, 0)


def run_grads(rows, hidden, gate_grad, up_grad, slot_grad, logits, shape):
    count, width = rows.shape
    steps = 4
    step = width // steps
    experts = logits.shape[2]
    blocks, planes, tail = shape[0] // steps, shape[1], shape[2:]
    column = pl.BlockSpec((count, step), lambda i: (0, i))
    whole = lambda value: pl.BlockSpec(value.shape, lambda i: (0,) * value.ndim)
    return pl.pallas_call(
        grads_kernel,
        grid=(steps,),
        in_specs=[column, whole(hidden), whole(gate_grad), whole(up_grad), column, whole(logits)],
        out_specs=[
            pl.BlockSpec((blocks, planes, 2) + tail, lambda i: (i, 0, 0, 0, 0)),
            pl.BlockSpec((blocks, planes) + tail, lambda i: (i, 0, 0, 0)),
            pl.BlockSpec((experts, step), lambda i: (0, i)),
        ],
        out_shape=[
            jax.ShapeDtypeStruct(shape[:2] + (2,) + tail, jnp.bfloat16),
            jax.ShapeDtypeStruct(shape, jnp.bfloat16),
            jax.ShapeDtypeStruct((experts, width), jnp.float32),
        ],
        compiler_params=params(FULL),
        cost_estimate=cost(6 * count * math.prod(shape), 12 << 20),
        name="expert_grads",
    )(rows, hidden, gate_grad, up_grad, slot_grad, logits)


def tables_kernel(place_ref, placement_ref, lengths_ref, facts_ref, cos_ref, sin_ref):
    holder = lax.fori_loop(
        0,
        placement_ref.shape[0],
        lambda i, total: total + jnp.where(placement_ref[i] == place_ref[1], i, 0),
        jnp.int32(0),
    )
    facts_ref[0] = place_ref[0]
    facts_ref[1] = place_ref[2]
    rows, lanes = cos_ref.shape
    row = lax.broadcasted_iota(jnp.int32, (rows, lanes), 0)
    start = jnp.zeros((rows, lanes), jnp.int32)
    end = jnp.int32(0)
    count = lengths_ref.shape[0]
    for j in range(count):
        end = end + lengths_ref[j, holder]
        facts_ref[3 + j] = end
        start = jnp.where(row >= end, end, start)
    facts_ref[2] = end
    half = HEAD_DIM // 2
    lane = lax.broadcasted_iota(jnp.int32, (rows, lanes), 1)
    index = jnp.bitwise_and(lane, half - 1).astype(jnp.float32)
    frequency = jnp.exp(-(2.0 * index / (2.0 * half)) * math.log(ROPE_BASE))
    angles = (row - start).astype(jnp.float32) * frequency
    cos_ref[...] = jnp.cos(angles)
    sine = jnp.sin(angles)
    sin_ref[...] = jnp.where(jnp.bitwise_and(lane, half) == 0, -sine, sine)


def make_tables(place, placement, lengths_t, rows):
    table = jax.ShapeDtypeStruct((rows, 128), jnp.float32)
    return pl.pallas_call(
        tables_kernel,
        in_specs=[SMEM, SMEM, SMEM],
        out_specs=[SMEM, VMEM, VMEM],
        out_shape=[
            jax.ShapeDtypeStruct((3 + lengths_t.shape[0],), jnp.int32),
            table,
            table,
        ],
        compiler_params=params(FULL),
        cost_estimate=cost(1 << 20, 1 << 18, rows * 256),
        name="tables",
    )(place, placement, lengths_t)


def turn(values, cos, sine):
    half = HEAD_DIM // 2
    lane = lax.broadcasted_iota(jnp.int32, cos.shape, 1)
    first = jnp.bitwise_and(lane, half) == 0
    pieces = []
    for c in range(values.shape[1] // 128):
        piece = values[:, c * 128 : (c + 1) * 128]
        other = jnp.where(first, pltpu.roll(piece, 128 - half, 1), pltpu.roll(piece, half, 1))
        pieces.append(piece * cos + other * sine)
    return jnp.concatenate(pieces, axis=1)


def allowed_pairs(facts_ref, rows):
    query = lax.broadcasted_iota(jnp.int32, (rows, rows), 0)
    key = lax.broadcasted_iota(jnp.int32, (rows, rows), 1)
    start = jnp.zeros((rows, rows), jnp.int32)
    for j in range(3, facts_ref.shape[0]):
        start = jnp.where(query >= facts_ref[j], facts_ref[j], start)
    return (key <= query) & (key >= start)


def pair_heads(values, g):
    chunk = values[:, 2 * g * HEAD_DIM : 2 * (g + 1) * HEAD_DIM]
    return jnp.concatenate([chunk[:, :HEAD_DIM], chunk[:, HEAD_DIM:]], axis=0)


def unpair_heads(values):
    rows = values.shape[0] // 2
    return jnp.concatenate([values[:rows], values[rows:]], axis=1)


def pair_scores(query, key, allowed):
    scores = dot(query, key, 1, 1) * (1.0 / HEAD_DIM)
    return jnp.where(jnp.concatenate([allowed, allowed], axis=0), scores, NEGATIVE)


def put_halves(ref, plane, own, away):
    width = ref.shape[1]
    ref[:, columns_of(plane, width, True)] = own
    ref[:, columns_of(plane, width, False)] = away


def inverse_norm(values):
    mean = jnp.mean(values * values, axis=1, keepdims=True)
    return lax.rsqrt(mean + EPSILON)


def attend_kernel(
    facts_ref,
    own_ref,
    away_ref,
    gain_ref,
    query_w_ref,
    key_w_ref,
    value_w_ref,
    output_w_ref,
    cos_ref,
    sin_ref,
    part_ref,
    normed_ref,
    query_ref,
    key_ref,
    value_ref,
    context_ref,
    total_ref,
    wide,
):
    put_halves(
        wide, facts_ref[0], own_ref[...].astype(jnp.float32), away_ref[...].astype(jnp.float32)
    )
    values = wide[...]
    rows = values.shape[0]
    normed = (values * inverse_norm(values) * gain_ref[...]).astype(jnp.bfloat16)
    normed_ref[...] = normed
    cos, sine = cos_ref[...], sin_ref[...]
    query = turn(dot(normed, query_w_ref[...]), cos, sine).astype(jnp.bfloat16)
    key = turn(dot(normed, key_w_ref[...]), cos, sine).astype(jnp.bfloat16)
    value = dot(normed, value_w_ref[...]).astype(jnp.bfloat16)
    query_ref[...] = query
    key_ref[...] = key
    value_ref[...] = value
    allowed = allowed_pairs(facts_ref, rows)
    live = lax.broadcasted_iota(jnp.int32, (rows, 2 * HEAD_DIM), 0) < facts_ref[2]
    pieces, totals = [], []
    for g in range(key.shape[1] // HEAD_DIM):
        place = slice(g * HEAD_DIM, (g + 1) * HEAD_DIM)
        scores = pair_scores(pair_heads(query, g), key[:, place], allowed)
        top = jnp.max(scores, axis=1, keepdims=True)
        terms = jnp.exp(scores - top)
        total = jnp.sum(terms, axis=1, keepdims=True)
        probs = (terms / total).astype(jnp.bfloat16)
        context = unpair_heads(dot(probs, value[:, place]))
        pieces.append(jnp.where(live, context, 0.0).astype(jnp.bfloat16))
        log_total = top + jnp.log(total)
        totals += [log_total[:rows], log_total[rows:]]
    context = jnp.concatenate(pieces, axis=1)
    context_ref[...] = context
    lane = lax.broadcasted_iota(jnp.int32, (rows, 128), 1)
    packed = jnp.zeros((rows, 128), jnp.float32)
    for h, log_total in enumerate(totals):
        packed = jnp.where(lane == h, log_total, packed)
    total_ref[...] = packed
    part_ref[...] = dot(context, output_w_ref[...]).astype(jnp.bfloat16)


def attend(facts, own, away, gain, query_w, key_w, value_w, output_w, cos, sine):
    rows = own.shape[0]
    width = 2 * own.shape[1]
    low = lambda columns: jax.ShapeDtypeStruct((rows, columns), jnp.bfloat16)
    return pl.pallas_call(
        attend_kernel,
        in_specs=[SMEM] + [VMEM] * 9,
        out_specs=[VMEM] * 7,
        out_shape=[
            low(width),
            low(width),
            low(query_w.shape[1]),
            low(key_w.shape[1]),
            low(value_w.shape[1]),
            low(query_w.shape[1]),
            jax.ShapeDtypeStruct((rows, 128), jnp.float32),
        ],
        scratch_shapes=[pltpu.VMEM((rows, width), jnp.float32)],
        compiler_params=params(FULL),
        cost_estimate=cost(8 * rows * width * width // 2, 8 << 20, rows * rows * 8),
        name="attend",
    )(facts, own, away, gain, query_w, key_w, value_w, output_w, cos, sine)


def mix_kernel(
    facts_ref, own_ref, away_ref, part_ref, recv_ref, gain_ref, residual_ref, mixed_ref, half_ref
):
    plane = facts_ref[0]
    put_halves(
        residual_ref, plane, own_ref[...].astype(jnp.float32), away_ref[...].astype(jnp.float32)
    )
    residual = residual_ref[...] + (
        part_ref[...].astype(jnp.float32) + recv_ref[...].astype(jnp.float32)
    )
    residual_ref[...] = residual
    mixed_ref[...] = (residual * inverse_norm(residual) * gain_ref[...]).astype(jnp.bfloat16)
    half_ref[...] = mixed_ref[:, columns_of(plane, residual.shape[1], True)]


def mix(facts, own, away, part, recv, gain):
    rows, width = part.shape
    return pl.pallas_call(
        mix_kernel,
        in_specs=[SMEM] + [VMEM] * 5,
        out_specs=[VMEM] * 3,
        out_shape=[
            jax.ShapeDtypeStruct((rows, width), jnp.float32),
            jax.ShapeDtypeStruct((rows, width), jnp.bfloat16),
            jax.ShapeDtypeStruct((rows, width // 2), jnp.bfloat16),
        ],
        compiler_params=params(FULL),
        cost_estimate=cost(rows * width * 8, 3 << 20),
        name="mix",
    )(facts, own, away, part, recv, gain)


def attend_back_kernel(
    facts_ref,
    mixed_ref,
    mixed_away_ref,
    cot_ref,
    cot_away_ref,
    residual_ref,
    own_ref,
    away_ref,
    gain_ref,
    expert_gain_ref,
    normed_ref,
    query_ref,
    key_ref,
    value_ref,
    context_ref,
    total_ref,
    query_w_ref,
    key_w_ref,
    value_w_ref,
    output_w_ref,
    cos_ref,
    sin_ref,
    router_ref,
    parts_ref,
    normed_own_ref,
    normed_away_ref,
    base_ref,
    inner_ref,
    wide,
):
    plane = facts_ref[0]
    own_columns = columns_of(plane, wide.shape[1], True)
    away_columns = columns_of(plane, wide.shape[1], False)
    rows, width = wide.shape

    put_halves(
        wide, plane, mixed_ref[...].astype(jnp.float32), mixed_away_ref[...].astype(jnp.float32)
    )
    mixed_grad = wide[...]
    put_halves(
        wide, plane, cot_ref[...].astype(jnp.float32), cot_away_ref[...].astype(jnp.float32)
    )
    residual = residual_ref[...]
    inverse = inverse_norm(residual)
    scaled = mixed_grad * expert_gain_ref[...]
    mean = jnp.mean(scaled * residual, axis=1, keepdims=True)
    residual_grad = (
        wide[...] + inverse * scaled - residual * (inverse * inverse * inverse * mean)
    )
    expert_gain_grad = 0.5 * jnp.sum(mixed_grad * residual * inverse, axis=0, keepdims=True)
    wide[...] = residual_grad
    base_ref[...] = wide[:, own_columns]
    low = residual_grad.astype(jnp.bfloat16)
    context = context_ref[...]
    columns = context.shape[1]
    parts_ref[:, :columns] = dot(low, context, 0, 0).astype(parts_ref.dtype)
    live = lax.broadcasted_iota(jnp.int32, (rows, columns), 0) < facts_ref[2]
    context_grad = jnp.where(live, dot(low, output_w_ref[...], 1, 1), 0.0).astype(jnp.bfloat16)

    query, key, value = query_ref[...], key_ref[...], value_ref[...]
    totals = total_ref[...]
    allowed = allowed_pairs(facts_ref, rows)
    scale = 1.0 / HEAD_DIM
    query_grads, key_grads, value_grads = [], [], []
    for g in range(key.shape[1] // HEAD_DIM):
        place = slice(g * HEAD_DIM, (g + 1) * HEAD_DIM)
        pair = pair_heads(query, g)
        pair_grad = pair_heads(context_grad, g)
        total = jnp.concatenate([totals[:, 2 * g : 2 * g + 1], totals[:, 2 * g + 1 : 2 * g + 2]])
        probs = jnp.exp(pair_scores(pair, key[:, place], allowed) - total)
        prob_grad = dot(pair_grad, value[:, place], 1, 1)
        inner = jnp.sum(probs * prob_grad, axis=1, keepdims=True)
        score_grad = (probs * (prob_grad - inner)).astype(jnp.bfloat16)
        query_grads.append(unpair_heads(dot(score_grad, key[:, place]) * scale))
        key_grads.append(dot(score_grad, pair, 0, 0) * scale)
        value_grads.append(dot(probs.astype(jnp.bfloat16), pair_grad, 0, 0))
    cos, sine = cos_ref[...], -sin_ref[...]
    query_grad = turn(jnp.concatenate(query_grads, axis=1), cos, sine).astype(jnp.bfloat16)
    key_grad = turn(jnp.concatenate(key_grads, axis=1), cos, sine).astype(jnp.bfloat16)
    value_grad = jnp.concatenate(value_grads, axis=1).astype(jnp.bfloat16)
    normed_t = normed_ref[...]
    start = columns
    for grad in (query_grad, key_grad, value_grad):
        size = grad.shape[1]
        parts_ref[:, start : start + size] = dot(normed_t, grad, 0, 0).astype(parts_ref.dtype)
        start += size
    normed_grad = (
        dot(query_grad, query_w_ref[...], 1, 1)
        + dot(key_grad, key_w_ref[...], 1, 1)
        + dot(value_grad, value_w_ref[...], 1, 1)
    )
    put_halves(
        wide, plane, own_ref[...].astype(jnp.float32), away_ref[...].astype(jnp.float32)
    )
    values = wide[...]
    product = normed_grad * values
    gain_grad = jnp.sum(product * inverse_norm(values), axis=0, keepdims=True)
    inner = jnp.sum(product * gain_ref[...], axis=1, keepdims=True)
    inner_ref[...] = jnp.broadcast_to(inner, (rows, 128)).T[: inner_ref.shape[0]]
    wide[...] = normed_grad
    normed_own_ref[...] = wide[:, own_columns]
    normed_away_ref[...] = wide[:, away_columns].astype(jnp.bfloat16)
    experts = router_ref.shape[0]
    rest = jnp.zeros((128 - experts - 2, width), jnp.float32)
    packed = jnp.concatenate([router_ref[...], gain_grad, expert_gain_grad, rest], axis=0)
    parts_ref[:, start : start + 128] = packed.T.astype(parts_ref.dtype)


def attend_back(facts, *values):
    mixed, query_w, key_w, value_w = values[0], values[15], values[16], values[17]
    rows, half = mixed.shape
    width = 2 * half
    columns = 2 * query_w.shape[1] + key_w.shape[1] + value_w.shape[1] + 128
    wide = lambda columns, kind: jax.ShapeDtypeStruct((rows, columns), kind)
    return pl.pallas_call(
        attend_back_kernel,
        in_specs=[SMEM] + [VMEM] * len(values),
        out_specs=[VMEM] * 5,
        out_shape=[
            jax.ShapeDtypeStruct((width, columns), jnp.bfloat16),
            wide(half, jnp.float32),
            wide(half, jnp.bfloat16),
            wide(half, jnp.float32),
            jax.ShapeDtypeStruct((8, rows), jnp.float32),
        ],
        scratch_shapes=[pltpu.VMEM((rows, width), jnp.float32)],
        compiler_params=params(FULL),
        cost_estimate=cost(16 * rows * width * half * 2, 14 << 20, rows * rows * 8),
        name="attend_back",
    )(facts, *values)


def finish_kernel(
    facts_ref,
    own_ref,
    away_ref,
    gain_ref,
    residual_ref,
    moe_ref,
    moe_recv_ref,
    moe_cross_ref,
    base_ref,
    normed_ref,
    normed_recv_ref,
    inner_ref,
    inner_recv_ref,
    out_ref,
):
    rows, half = own_ref.shape
    own_columns = columns_of(facts_ref[0], 2 * half, True)
    own = own_ref[...].astype(jnp.float32)
    away = away_ref[...].astype(jnp.float32)
    total = jnp.sum(own * own, axis=1, keepdims=True) + jnp.sum(away * away, axis=1, keepdims=True)
    inverse = lax.rsqrt(total / (2 * half) + EPSILON)
    inner = (inner_ref[0:1, :] + inner_recv_ref[0:1, :]) / (2 * half)
    inner = jnp.broadcast_to(inner, (128, rows)).T[:, :1]
    normed = normed_ref[...] + normed_recv_ref[...].astype(jnp.float32)
    grad = (
        base_ref[...]
        + inverse * normed * gain_ref[:, own_columns]
        - own * (inverse * inverse * inverse * inner)
    )
    moe = (
        moe_ref[...]
        + moe_recv_ref[...].astype(jnp.float32)
        + moe_cross_ref[...].astype(jnp.float32)
    )
    out_ref[:, :half] = (residual_ref[:, own_columns] + moe).astype(out_ref.dtype)
    out_ref[:, half:] = grad.astype(out_ref.dtype)


def finish(facts, *values):
    rows, half = values[0].shape
    return pl.pallas_call(
        finish_kernel,
        in_specs=[SMEM] + [VMEM] * len(values),
        out_specs=VMEM,
        out_shape=jax.ShapeDtypeStruct((rows, 2 * half), jnp.bfloat16),
        compiler_params=params(FULL),
        cost_estimate=cost(rows * half * 16, 4 << 20),
        name="finish",
    )(facts, *values)


def local(
    inputs,
    cotangent,
    attn_gain,
    expert_gain,
    query_weight,
    key_weight,
    value_weight,
    output_weight,
    router_weight,
    gate_weight,
    up_weight,
    down_weight,
    routes,
    lengths,
    placement,
):
    row_count, top_count = routes.shape
    expert_count = router_weight.shape[1]
    capacity = row_count * top_count // expert_count
    kv_local = key_weight.shape[1] // HEAD_DIM
    heads_local = query_weight.shape[1] // HEAD_DIM
    group = heads_local // kv_local
    scale = 1.0 / HEAD_DIM
    width_half = inputs.shape[1]
    width = 2 * width_half
    plane = lax.axis_index("tensor")
    devices = lax.axis_size("dp")
    dp_index = lax.axis_index("dp")
    members = expert_count // 2
    near = members // 2
    clusters = devices // members
    member = dp_index % members
    expert = 2 * member + plane
    inside = [[c * members + m for m in range(members)] for c in range(clusters)]
    across = [[c * members + m for c in range(clusters)] for m in range(members)]

    def cross(values):
        return lax.ppermute(values, "dp", [(i, i ^ near) for i in range(devices)])

    def spread(blocks):
        return [blocks[0]] + [
            lax.ppermute(blocks[s], "dp", [(i, i ^ s) for i in range(devices)])
            for s in range(1, near)
        ]

    def halves(values, axis):
        size = values.shape[axis] // 2
        return (
            lax.dynamic_slice_in_dim(values, plane * size, size, axis),
            lax.dynamic_slice_in_dim(values, (1 - plane) * size, size, axis),
        )

    def join(own, other, axis):
        first = jnp.where(plane == 0, own, other)
        second = jnp.where(plane == 0, other, own)
        return jnp.concatenate([first, second], axis=axis)

    def add_planes(part):
        low = part.astype(jnp.bfloat16)
        return low.astype(jnp.float32) + swap_tensor(low).astype(jnp.float32)

    routes_t = routes.T
    away = swap_tensor(inputs)
    partner_t = cross(routes_t)
    cot_cross = cross(cotangent)
    cot_away = swap_tensor(cotangent)
    cot_cross_away = swap_tensor(cot_cross)
    place = jnp.stack([plane, dp_index, member]).astype(jnp.int32)
    facts, cos_table, sin_table = make_tables(place, placement, lengths.T, row_count)
    gain_one, gain_two = attn_gain[None], expert_gain[None]
    attn_part, normed, query, key, value, context, log_total = attend(
        facts,
        inputs,
        away,
        gain_one,
        query_weight,
        key_weight,
        value_weight,
        output_weight,
        cos_table,
        sin_table,
    )

    def to_owner(values):
        if clusters == 1:
            owned = lax.all_to_all(
                values, ("dp", "tensor"), split_axis=0, concat_axis=0, tiled=True
            )
            return owned.reshape((devices, 2) + owned.shape[1:])
        by_plane = values.reshape((members, 2) + values.shape[1:])
        own_w = lax.dynamic_index_in_dim(by_plane, plane, 1, keepdims=False)
        other_w = swap_tensor(lax.dynamic_index_in_dim(by_plane, 1 - plane, 1, keepdims=False))
        owned = jnp.stack(
            [jnp.where(plane == 0, own_w, other_w), jnp.where(plane == 0, other_w, own_w)], axis=1
        )
        owned = lax.all_to_all(
            owned, "dp", split_axis=0, concat_axis=0, tiled=True, axis_index_groups=inside
        )
        owned = lax.all_gather(owned, "dp", axis=0, tiled=True, axis_index_groups=across)
        owned = owned.reshape((members, clusters) + owned.shape[1:])
        owned = jnp.moveaxis(owned, 1, -3)
        return owned.reshape(owned.shape[:-3] + (-1, owned.shape[-1]))

    def from_owner(values):
        if clusters == 1:
            return lax.all_to_all(
                values.reshape((2 * devices,) + values.shape[2:]),
                ("dp", "tensor"),
                split_axis=0,
                concat_axis=0,
                tiled=True,
            )
        values = values.reshape(values.shape[:-2] + (clusters, -1, values.shape[-1]))
        values = jnp.moveaxis(values, -3, 1)
        values = values.reshape((devices,) + values.shape[2:])
        values = lax.psum_scatter(
            values, "dp", scatter_dimension=0, tiled=True, axis_index_groups=across
        )
        values = lax.all_to_all(
            values, "dp", split_axis=0, concat_axis=0, tiled=True, axis_index_groups=inside
        )
        own_g = lax.dynamic_index_in_dim(values, plane, 1, keepdims=False)
        other_g = swap_tensor(lax.dynamic_index_in_dim(values, 1 - plane, 1, keepdims=False))
        values = jnp.stack(
            [jnp.where(plane == 0, own_g, other_g), jnp.where(plane == 0, other_g, own_g)], axis=1
        )
        return values.reshape((expert_count,) + values.shape[2:])

    owned = to_owner(
        after(
            jnp.stack([gate_weight, up_weight, jnp.swapaxes(down_weight, 1, 2)], axis=1),
            away,
            partner_t,
            cot_away,
            cot_cross,
        )
    )

    hot, cot_blocks = dispatch_cot(
        facts,
        routes_t,
        partner_t,
        cotangent,
        cot_cross,
        cot_away,
        cot_cross_away,
        near,
        capacity,
        expert_count,
    )
    cot_blocks = spread(cot_blocks)

    def combine(hot, blocks):
        mine, mine_away, others, others_away = combine_rows(facts, hot, blocks, capacity)
        others = others + swap_tensor(others_away).astype(jnp.float32)
        return mine, swap_tensor(mine_away), cross(others.astype(jnp.bfloat16))

    residual, mixed_rows, mixed_half = mix(
        facts, inputs, away, attn_part, swap_tensor(attn_part), gain_two
    )
    mixed_cross = cross(mixed_half)
    mixed_away = swap_tensor(mixed_cross)
    row_blocks = spread(
        dispatch_rows(
            facts, after(hot, *cot_blocks[1:7]), mixed_rows, mixed_cross, mixed_away, near, capacity
        )
    )

    back_blocks, moe_blocks, kept = run_expert(
        facts, row_blocks, cot_blocks, owned, router_weight.T
    )
    back_blocks = spread(back_blocks)
    pair_part, down_part, router_part = run_grads(
        *kept, (members, 2, width // members, gate_weight.shape[2])
    )
    down_share = from_owner(down_part)
    moe_blocks = spread(moe_blocks)
    mine, mine_recv, mine_cross = combine(after(hot, down_share), back_blocks)
    mixed_half = mine + mine_recv.astype(jnp.float32) + mine_cross.astype(jnp.float32)
    mixed_half = mixed_half.astype(jnp.bfloat16)
    mixed_away = swap_tensor(mixed_half)
    pair_share = from_owner(after(pair_part, mixed_half))
    moe_parts = combine(hot, moe_blocks)

    parts, normed_own, normed_away, base_half, inner = attend_back(
        facts,
        mixed_half,
        mixed_away,
        cotangent,
        cot_away,
        after(residual, *moe_blocks),
        inputs,
        away,
        gain_one,
        gain_two,
        normed,
        query,
        key,
        value,
        context,
        log_total,
        query_weight,
        key_weight,
        value_weight,
        output_weight,
        cos_table,
        sin_table,
        router_part,
    )
    share = lax.psum_scatter(parts, "dp", scatter_dimension=0, tiled=True)
    cuts = [context.shape[1]]
    for w in (query_weight, key_weight, value_weight):
        cuts.append(cuts[-1] + w.shape[1])
    small = share[:, cuts[3] :]
    small = small.astype(jnp.float32) + swap_tensor(small).astype(jnp.float32)
    output_part = share[:, : cuts[0]].T.astype(jnp.float32)
    query_part = share[:, cuts[0] : cuts[1]].astype(jnp.float32)
    key_part = share[:, cuts[1] : cuts[2]].astype(jnp.float32)
    value_part = share[:, cuts[2] : cuts[3]].astype(jnp.float32)
    router_share = small[:, :expert_count]
    attn_gain_part = small[:, expert_count]
    expert_gain_part = small[:, expert_count + 1]

    gate_w_part = pair_share[:, 0].astype(jnp.float32)
    up_w_part = pair_share[:, 1].astype(jnp.float32)
    down_w_part = jnp.swapaxes(down_share, 1, 2).astype(jnp.float32)

    piece_rows = row_count // devices
    moved = finish(
        facts,
        inputs,
        away,
        gain_one,
        residual,
        *moe_parts,
        base_half,
        normed_own,
        swap_tensor(normed_away),
        inner,
        swap_tensor(inner),
    )
    moved = after(moved, pair_share)
    moved = lax.all_to_all(
        moved.reshape(devices, piece_rows, width), "dp", split_axis=0, concat_axis=0, tiled=True
    )
    moved = jnp.take(moved, placement, axis=0)
    moved = lax.all_to_all(moved, "dp", split_axis=0, concat_axis=0, tiled=True)
    moved = moved.reshape(row_count, width)
    outputs = moved[:, :width_half]
    input_result = moved[:, width_half:].astype(jnp.float32)
    return (
        outputs,
        input_result,
        attn_gain_part,
        expert_gain_part,
        query_part,
        key_part,
        value_part,
        output_part,
        router_share,
        gate_w_part,
        up_w_part,
        down_w_part,
    )


def solution(mesh):
    in_specs = (
        P("dp", "tensor"),
        P("dp", "tensor"),
        P(),
        P(),
        P(None, "tensor"),
        P(None, "tensor"),
        P(None, "tensor"),
        P("tensor", None),
        P(),
        P(None, "dp", "tensor"),
        P(None, "dp", "tensor"),
        P(None, "tensor", "dp"),
        P("dp", None),
        P(),
        P(),
    )
    out_specs = (
        P("dp", "tensor"),
        P("dp", "tensor"),
        P("dp"),
        P("dp"),
        P("dp", "tensor"),
        P("dp", "tensor"),
        P("dp", "tensor"),
        P("tensor", "dp"),
        P("dp", None),
        P(None, "dp", "tensor"),
        P(None, "dp", "tensor"),
        P(None, "tensor", "dp"),
    )
    return jax.shard_map(local, mesh=mesh, in_specs=in_specs, out_specs=out_specs, check_vma=False)
```
